128 devices in a mesh: layer: 8 (over z, core), energy: 4 (over y), momentum: 4 (over x).
Axes of the slice: x: 4, y: 4, z: 4, core: 2. Of those that a mesh axis runs over, the one named last changes fastest.
Arguments:
- diag_blocks: float32 [4, 16, 4, 2, 384, 384], P('momentum', 'layer', 'energy'), may hold values from -1 to 5
- couplings: float32 [4, 16, 2, 384, 384], P('momentum', 'layer'), may hold values from -0.15625 to 0.15625
- phonon_matrix: float32 [4, 4], replicated, may hold values from -3 to 3
- mode_strength: float32 [3], replicated, may hold values from 0.5 to 2
- transfer_mode: int32 [4], replicated, may hold values from 0 to 2, as said below
- energy_offset: int32 [3], replicated, may hold values from 0 to 1, as said below
Outputs:
- self_energy: float32 [4, 8, 4, 2, 384, 384], P('momentum', 'layer', 'energy')
The draws below stay inside these ranges and needn't reach their ends.
Inputs may be any that keep to these rules, and one draw needn't show every extreme that they name: `transfer_mode`: every one of the 3 modes is the mode of some transfer. `energy_offset`: some mode has offset 0 and some mode has offset 1.
All inputs are finite; a program needn't handle non-finite values.
Results may differ from the reference program's by a relative error of at most 0.00011.
Values sent between devices are 32-bit elements; how exact they have to be, the bound alone decides.
No kernel may reach another device: no remote copies, remote signals or barrier semaphores. Data moves between devices by JAX's collectives and lax.ppermute only.
A program may use at most 64 MiB of HBM per device.

```python
import math
from functools import partial
import jax
import jax.numpy as jnp
from jax import lax

B = 384
MODES = 3
LAYERS = 16
NE = 4
NK = 4
OFFMAX = 1


def draw_diag_blocks(key, part):
    base = jax.random.fold_in(key, 101)
    first_key, second_key, third_key = jax.random.split(base, 3)
    off_scale = 0.4 * math.sqrt(2.0) / math.sqrt(B)
    real_diag = jnp.exp(jax.random.uniform(first_key, (NK, LAYERS, NE, B), jnp.float32, math.log(2.0), math.log(4.0)))
    imag_diag = jax.random.uniform(second_key, (NK, LAYERS, NE, B), jnp.float32, 0.6, 1.2)
    noise = jnp.clip(jax.random.normal(third_key, (NK, LAYERS, NE, 2, B, B), jnp.float32), -4.0, 4.0) * off_scale
    noise_real = noise[..., 0, :, :]
    noise_imag = noise[..., 1, :, :]
    herm_real = 0.5 * (noise_real + jnp.swapaxes(noise_real, -1, -2))
    herm_imag = 0.5 * (noise_imag - jnp.swapaxes(noise_imag, -1, -2))
    identity = jnp.eye(B, dtype=jnp.float32)
    block_real = herm_real + identity * real_diag[..., None]
    block_imag = herm_imag + identity * imag_diag[..., None]
    return jnp.stack([block_real, block_imag], axis=-3).astype(jnp.float32)


def draw_transfer_mode(key, part):
    base = jax.random.fold_in(key, 202)
    return jax.random.permutation(base, jnp.arange(NK, dtype=jnp.int32) % MODES).astype(jnp.int32)


def draw_energy_offset(key, part):
    base = jax.random.fold_in(key, 303)
    first_key, second_key = jax.random.split(base, 2)
    values = jax.random.randint(first_key, (MODES,), 0, OFFMAX + 1, dtype=jnp.int32)
    order = jax.random.permutation(second_key, MODES)
    values = values.at[order[0]].set(0)
    values = values.at[order[1]].set(OFFMAX)
    return values.astype(jnp.int32)


def level_of(stream_key, dims, pieces, low, largest):
    gain, own = 1.0, jax.random.fold_in(stream_key, 6)
    for axis_at, parts in pieces:
        draws = jnp.exp(jax.random.uniform(jax.random.fold_in(own, axis_at), (parts,), jnp.float32, low / len(pieces), largest / len(pieces)))
        gain = gain * jnp.repeat(draws, dims[axis_at] // parts).reshape([-1 if axis == axis_at else 1 for axis in range(len(dims))])
    return gain


def gaussian(stream_key, dims, deviation, reach, pieces=(), kind=jnp.bfloat16):
    values = deviation * jax.random.normal(stream_key, dims, jnp.float32)
    if pieces:
        values = values * level_of(stream_key, dims, pieces, -0.22, 0.18)
    return jnp.clip(values, -reach, reach).astype(kind)


def setup_inputs(seed: int = 0) -> dict:
    streams_of = jax.random.split(jax.random.key(seed), 7)
    diag_blocks = draw_diag_blocks(jax.random.fold_in(streams_of[6], 71), 0)
    couplings = gaussian(streams_of[1], (NK, LAYERS, 2, B, B), (4 * B) ** -0.5, 0.15625, ((0, 4), (1, 8)), jnp.float32)
    phonon_matrix = gaussian(streams_of[2], (NE, NE), NE ** -0.5, 3.0, (), jnp.float32)
    mode_strength = jnp.clip(jnp.exp(jax.random.uniform(streams_of[3], (MODES,), jnp.float32, math.log(0.5), math.log(2.0))), 0.5, 2.0)
    transfer_mode = draw_transfer_mode(jax.random.fold_in(streams_of[6], 71), 0)
    energy_offset = draw_energy_offset(jax.random.fold_in(streams_of[6], 71), 0)
    return dict(diag_blocks=diag_blocks, couplings=couplings, phonon_matrix=phonon_matrix, mode_strength=mode_strength, transfer_mode=transfer_mode, energy_offset=energy_offset)


def complex_product(left, right):
    product = partial(jnp.matmul, precision=lax.Precision.HIGHEST)
    real_part = product(left[..., 0, :, :], right[..., 0, :, :]) - product(left[..., 1, :, :], right[..., 1, :, :])
    imag_part = product(left[..., 0, :, :], right[..., 1, :, :]) + product(left[..., 1, :, :], right[..., 0, :, :])
    return jnp.stack([real_part, imag_part], axis=-3)


def adjoint(matrix):
    return jnp.stack([jnp.swapaxes(matrix[..., 0, :, :], -1, -2), -jnp.swapaxes(matrix[..., 1, :, :], -1, -2)], axis=-3)


def refined_inverse(matrix):
    real_diag = jnp.diagonal(matrix[..., 0, :, :], axis1=-2, axis2=-1)
    imag_diag = jnp.diagonal(matrix[..., 1, :, :], axis1=-2, axis2=-1)
    modulus = real_diag * real_diag + imag_diag * imag_diag
    inv_real = real_diag / modulus
    inv_imag = -imag_diag / modulus
    block_order = matrix.shape[-1]
    identity = jnp.eye(block_order, dtype=jnp.float32)
    scaled_real = matrix[..., 0, :, :] * inv_real[..., None, :] - matrix[..., 1, :, :] * inv_imag[..., None, :]
    scaled_imag = matrix[..., 0, :, :] * inv_imag[..., None, :] + matrix[..., 1, :, :] * inv_real[..., None, :]
    resid_real = 2.0 * identity - scaled_real
    resid_imag = -scaled_imag
    first_real = inv_real[..., :, None] * resid_real - inv_imag[..., :, None] * resid_imag
    first_imag = inv_real[..., :, None] * resid_imag + inv_imag[..., :, None] * resid_real
    first = jnp.stack([first_real, first_imag], axis=-3)
    two_identity = jnp.stack([2.0 * identity, jnp.zeros_like(identity)], axis=0)
    residual = two_identity - complex_product(matrix, first)
    return complex_product(first, residual)


def shift_down(values):
    return jnp.concatenate([jnp.zeros_like(values[:1]), values[:-1]], axis=0)


def shift_up(values):
    return jnp.concatenate([values[1:], jnp.zeros_like(values[:1])], axis=0)


def reduce_momentum(operands):
    diag_one, coupling_one = operands
    even_diag = diag_one[0::2]
    odd_diag = diag_one[1::2]
    even_coupling = coupling_one[0::2][:, None]
    odd_coupling = coupling_one[1::2][:, None]
    odd_inverse = refined_inverse(odd_diag)
    even_adjoint = adjoint(even_coupling)
    odd_adjoint = adjoint(odd_coupling)
    left_even = complex_product(even_coupling, odd_inverse)
    left_odd = complex_product(odd_adjoint, odd_inverse)
    own_term = complex_product(left_even, even_adjoint)
    edge_term = complex_product(left_odd, odd_coupling)
    upper = -complex_product(left_even, odd_coupling)
    lower = -complex_product(left_odd, even_adjoint)
    reduced = even_diag - own_term - shift_down(edge_term)
    reduced_inverse = refined_inverse(reduced)
    lower_term = complex_product(complex_product(lower, reduced_inverse), upper)
    upper_term = complex_product(complex_product(upper, shift_up(reduced_inverse)), lower)
    twice = reduced - upper_term - shift_down(lower_term)
    return refined_inverse(twice)


def reference(diag_blocks, couplings, phonon_matrix, mode_strength, transfer_mode, energy_offset):
    greens = lax.map(reduce_momentum, (diag_blocks, couplings))
    folded = jnp.einsum('ef,kjfcrb->kjecrb', phonon_matrix, greens, precision=lax.Precision.HIGHEST)
    energies = jnp.arange(NE, dtype=jnp.int32)
    target = energies[:, None]
    source = energies[None, :]
    total = jnp.zeros_like(folded)
    for transfer in range(NK):
        mode = transfer_mode[transfer]
        offset = energy_offset[mode]
        strength = mode_strength[mode]
        kernel = strength * ((source == target - offset).astype(jnp.float32) + (source == target + offset).astype(jnp.float32))
        total = total + jnp.einsum('ef,kjfcrb->kjecrb', kernel, jnp.roll(folded, transfer, axis=0), precision=lax.Precision.HIGHEST)
    return total
```

```python
import jax
import jax.numpy as jnp
from jax import lax
from jax.experimental import pallas as pl
from jax.experimental.pallas import tpu as pltpu
from jax.sharding import PartitionSpec as P

F32 = jnp.float32
BF16 = jnp.bfloat16


def from_behind(block, axis, distance):
    devices = range(lax.axis_size(axis))
    route = [(i - distance, i) for i in devices if i - distance in devices]
    return lax.ppermute(block, axis, route)


def split(value):
    high = value.astype(BF16)
    return high, (value - high.astype(F32)).astype(BF16)


def put_left(left_high, left_low, rows, real, imag):
    n = real.shape[-1]
    for part, at in ((real, 0), (imag, n)):
        high, low = split(part)
        left_high[rows, at : at + n] = high
        left_low[rows, at : at + n] = low


def put_right(right_high, right_low, real, imag):
    n = real.shape[-1]
    for ref, r, i in zip((right_high, right_low), split(real), split(imag)):
        ref[0:n, 0:n] = r
        ref[0:n, n : 2 * n] = i
        ref[n : 2 * n, 0:n] = -i
        ref[n : 2 * n, n : 2 * n] = r


def product(out, rows, left_high, left_low, right_high, right_low):
    width = right_high.shape[1]
    step = 256
    for at in range(0, width, step):
        columns = slice(at, at + step)
        high = right_high[:, columns]
        low = right_low[:, columns]
        lh = left_high[rows, :]
        out[rows, columns] = (
            jnp.dot(lh, high, preferred_element_type=F32)
            + jnp.dot(lh, low, preferred_element_type=F32)
            + jnp.dot(left_low[rows, :], high, preferred_element_type=F32)
        )


def inverse_diagonal(real, imag):
    n = real.shape[-1]
    rows, columns = [], []
    on = lax.broadcasted_iota(jnp.int32, (128, 128), 0) == lax.broadcasted_iota(
        jnp.int32, (128, 128), 1
    )
    for at in range(0, n, 128):
        s = slice(at, at + 128)
        tiles = [jnp.where(on, part[s, s], 0.0) for part in (real, imag)]
        columns.append([jnp.sum(t, axis=1, keepdims=True) for t in tiles])
        rows.append([jnp.sum(t, axis=0, keepdims=True) for t in tiles])
    result = []
    for pieces, axis in ((rows, 1), (columns, 0)):
        dr = jnp.concatenate([p[0] for p in pieces], axis=axis)
        di = jnp.concatenate([p[1] for p in pieces], axis=axis)
        modulus = dr * dr + di * di
        result += [dr / modulus, -di / modulus]
    return result


def refined_inverse(real, imag, scratch):
    left_high, left_low, right_high, right_low, out = scratch
    n = real.shape[-1]
    rows = slice(0, n)
    row_real, row_imag, col_real, col_imag = inverse_diagonal(real, imag)
    eye = (
        lax.broadcasted_iota(jnp.int32, (n, n), 0) == lax.broadcasted_iota(jnp.int32, (n, n), 1)
    ).astype(F32)
    m_real = real * row_real - imag * row_imag - eye
    m_imag = real * row_imag + imag * row_real
    put_left(left_high, left_low, rows, m_real, m_imag)
    put_right(right_high, right_low, m_real, m_imag)
    product(out, rows, left_high, left_low, right_high, right_low)
    t_real = out[rows, 0:n]
    t_imag = out[rows, n : 2 * n]
    put_right(right_high, right_low, t_real, t_imag)
    q_real = eye - m_real + t_real
    q_imag = t_imag - m_imag
    product(out, rows, left_high, left_low, right_high, right_low)
    q_real = q_real - out[rows, 0:n]
    q_imag = q_imag - out[rows, n : 2 * n]
    return col_real * q_real - col_imag * q_imag, col_real * q_imag + col_imag * q_real


def odd_kernel(odd, coupling, inverse, left_odd, edge, *scratch):
    left_high, left_low, right_high, right_low, out = scratch
    n = odd.shape[-1]
    rows = slice(0, n)
    real, imag = refined_inverse(odd[0], odd[1], scratch)
    inverse[:, 0:n] = real
    inverse[:, n : 2 * n] = imag
    put_right(right_high, right_low, real, imag)
    put_left(left_high, left_low, rows, coupling[0].T, -coupling[1].T)
    product(left_odd, rows, left_high, left_low, right_high, right_low)
    put_left(left_high, left_low, rows, left_odd[:, 0:n], left_odd[:, n : 2 * n])
    put_right(right_high, right_low, coupling[0], coupling[1])
    product(edge, rows, left_high, left_low, right_high, right_low)


def coupling_kernel(inverse, left_odd, even, coupling, before, upper, lower, *scratch):
    left_high, left_low, right_high, right_low, out = scratch
    n = even.shape[-1]
    rows, more = slice(0, n), slice(n, 2 * n)
    put_left(left_high, left_low, rows, coupling[0, 0], coupling[0, 1])
    put_right(right_high, right_low, inverse[:, 0:n], inverse[:, n : 2 * n])
    product(out, rows, left_high, left_low, right_high, right_low)
    put_left(left_high, left_low, rows, out[rows, 0:n], out[rows, n : 2 * n])
    put_left(left_high, left_low, more, left_odd[:, 0:n], left_odd[:, n : 2 * n])
    put_right(right_high, right_low, coupling[1, 0], coupling[1, 1])
    product(out, rows, left_high, left_low, right_high, right_low)
    upper[...] = -out[rows, :]
    put_right(right_high, right_low, coupling[0, 0].T, -coupling[0, 1].T)
    product(out, slice(0, 2 * n), left_high, left_low, right_high, right_low)
    lower[...] = -out[more, :]
    before[:, 0:n] = even[0] - out[rows, 0:n]
    before[:, n : 2 * n] = even[1] - out[rows, n : 2 * n]


def reduced_kernel(before, arrived, reduced, inverse, *scratch):
    n = before.shape[0]
    real = before[:, 0:n] - arrived[:, 0:n]
    imag = before[:, n : 2 * n] - arrived[:, n : 2 * n]
    reduced[:, 0:n] = real
    reduced[:, n : 2 * n] = imag
    real, imag = refined_inverse(real, imag, scratch)
    inverse[:, 0:n] = real
    inverse[:, n : 2 * n] = imag


def term_kernel(first, middle, last, term, *scratch):
    left_high, left_low, right_high, right_low, out = scratch
    n = first.shape[0]
    rows = slice(0, n)
    put_left(left_high, left_low, rows, first[:, 0:n], first[:, n : 2 * n])
    put_right(right_high, right_low, middle[:, 0:n], middle[:, n : 2 * n])
    product(out, rows, left_high, left_low, right_high, right_low)
    put_left(left_high, left_low, rows, out[rows, 0:n], out[rows, n : 2 * n])
    put_right(right_high, right_low, last[:, 0:n], last[:, n : 2 * n])
    product(term, rows, left_high, left_low, right_high, right_low)


def greens_kernel(reduced, upper_term, lower_term, greens, *scratch):
    n = reduced.shape[0]
    real = reduced[:, 0:n] - upper_term[:, 0:n] - lower_term[:, 0:n]
    imag = reduced[:, n : 2 * n] - upper_term[:, n : 2 * n] - lower_term[:, n : 2 * n]
    real, imag = refined_inverse(real, imag, scratch)
    greens[0] = real
    greens[1] = imag


def mix_kernel(phonon, strength, transfer, offset, blocks, mixed):
    energies, momenta, depth, width = blocks.shape
    stay, move = [], []
    for q in range(momenta):
        mode = transfer[q]
        weight = strength[mode]
        still = offset[mode] == 0
        stay.append(jnp.where(still, 2.0 * weight, 0.0))
        move.append(jnp.where(still, 0.0, weight))
    fold = [[phonon[e, f] for f in range(energies)] for e in range(energies)]
    for at in range(0, width, 128):
        columns = slice(at, at + 128)

        def rows_of(i, carry):
            rows = pl.ds(pl.multiple_of(i * 8, 8), 8)
            folded = []
            for k in range(momenta):
                g = [blocks[f, k, rows, columns] for f in range(energies)]
                folded.append(
                    [sum(fold[e][f] * g[f] for f in range(energies)) for e in range(energies)]
                )
            for k in range(momenta):
                moved = [
                    sum(move[q] * folded[(k - q) % momenta][e] for q in range(momenta))
                    for e in range(energies)
                ]
                for e in range(energies):
                    total = sum(stay[q] * folded[(k - q) % momenta][e] for q in range(momenta))
                    if e > 0:
                        total = total + moved[e - 1]
                    if e + 1 < energies:
                        total = total + moved[e + 1]
                    mixed[e, k, rows, columns] = total
            return carry

        lax.fori_loop(0, depth // 8, rows_of, 0)


def call(kernel, outs, operands, specs=None, products=0, tall=1, wide=True):
    n = operands[0].shape[-2]
    whole = pl.BlockSpec(memory_space=pltpu.VMEM)
    scratch = [
        pltpu.VMEM((tall * n, 2 * n), BF16),
        pltpu.VMEM((tall * n, 2 * n), BF16),
        pltpu.VMEM((2 * n, 2 * n), BF16),
        pltpu.VMEM((2 * n, 2 * n), BF16),
        pltpu.VMEM((tall * n, 2 * n), F32),
    ]
    return pl.pallas_call(
        kernel,
        out_shape=[jax.ShapeDtypeStruct(s, F32) for s in outs],
        grid=(1,),
        in_specs=specs or [pl.BlockSpec(o.shape, lambda i, r=o.ndim: (0,) * r) for o in operands],
        out_specs=[pl.BlockSpec(s, lambda i, r=len(s): (0,) * r) for s in outs],
        scratch_shapes=scratch,
        compiler_params=pltpu.CompilerParams(vmem_limit_bytes=40 * 1024 * 1024),
        cost_estimate=pl.CostEstimate(
            flops=products * 24 * n**3,
            bytes_accessed=8 * n * n * (len(outs) + len(operands)),
            transcendentals=0,
        ),
    )(*operands)


def body(diag_blocks, couplings, phonon_matrix, mode_strength, transfer_mode, energy_offset):
    n = diag_blocks.shape[-1]
    wide = (n, 2 * n)

    def diag(which):
        return pl.BlockSpec((None, None, None, 2, n, n), lambda i: (0, which, 0, 0, 0, 0))

    def whole(shape):
        return pl.BlockSpec(shape, lambda i: (0,) * len(shape))

    odd_coupling = pl.BlockSpec((None, None, 2, n, n), lambda i: (0, 1, 0, 0, 0))
    both = pl.BlockSpec((None, 2, 2, n, n), lambda i: (0, 0, 0, 0, 0))
    inverse, left_odd, edge = call(
        odd_kernel, [wide] * 3, (diag_blocks, couplings), [diag(1), odd_coupling], 4
    )
    arrived = from_behind(edge, "layer", 1)
    before, upper, lower = call(
        coupling_kernel,
        [wide] * 3,
        (inverse, left_odd, diag_blocks, couplings),
        [whole(wide), whole(wide), diag(0), both],
        4,
        tall=2,
    )
    reduced, reduced_inverse = call(reduced_kernel, [wide] * 2, (before, arrived), products=2)
    neighbour = from_behind(reduced_inverse, "layer", -1)
    (lower_term,) = call(term_kernel, [wide], (lower, reduced_inverse, upper), products=2)
    from_below = from_behind(lower_term, "layer", 1)
    (upper_term,) = call(term_kernel, [wide], (upper, neighbour, lower), products=2)
    (greens,) = call(greens_kernel, [(2, n, n)], (reduced, upper_term, from_below), products=2)
    energies, momenta = lax.axis_size("energy"), lax.axis_size("momentum")
    group = energies * momenta
    depth = 2 * n // group
    axes = ("energy", "momentum")
    spread = lax.all_to_all(
        greens.reshape(group, depth, n), axes, split_axis=0, concat_axis=0, tiled=True
    )
    block = (energies, momenta, depth, n)
    small = pl.BlockSpec(memory_space=pltpu.SMEM)
    mixed = pl.pallas_call(
        mix_kernel,
        out_shape=jax.ShapeDtypeStruct(block, F32),
        grid=(1,),
        in_specs=[small] * 4 + [whole(block)],
        out_specs=whole(block),
    )(phonon_matrix, mode_strength, transfer_mode, energy_offset, spread.reshape(block))
    returned = lax.all_to_all(
        mixed.reshape(group, depth, n), axes, split_axis=0, concat_axis=0, tiled=True
    )
    return returned.reshape(1, 1, 1, 2, n, n)


def solution(mesh):
    return jax.shard_map(
        body,
        mesh=mesh,
        in_specs=(
            P("momentum", "layer", "energy", None, None, None),
            P("momentum", "layer", None, None, None),
            P(),
            P(),
            P(),
            P(),
        ),
        out_specs=P("momentum", "layer", "energy", None, None, None),
        check_vma=False,
    )
```

```python
import jax
import jax.numpy as jnp
from jax import lax
from jax.experimental import pallas as pl
from jax.experimental.pallas import tpu as pltpu
from jax.sharding import PartitionSpec as P

F32 = jnp.float32
BF16 = jnp.bfloat16


def split(value):
    high = value.astype(BF16)
    return high, (value - high.astype(F32)).astype(BF16)


def put_left(left, rows, real, imag):
    n = real.shape[-1]
    for part, at in ((real, 0), (imag, n)):
        for ref, value in zip(left, split(part)):
            ref[rows, at : at + n] = value


def put_right(right, real, imag):
    n = real.shape[-1]
    for ref, r, i in zip(right, split(real), split(imag)):
        ref[0:n, 0:n] = r
        ref[0:n, n : 2 * n] = i
        ref[n : 2 * n, 0:n] = -i
        ref[n : 2 * n, n : 2 * n] = r


def product(out, left, right):
    step = 256
    for at in range(0, right[0].shape[1], step):
        columns = slice(at, at + step)
        high = right[0][:, columns]
        low = right[1][:, columns]
        lh = left[0][...]
        out[:, columns] = (
            jnp.dot(lh, high, preferred_element_type=F32)
            + jnp.dot(lh, low, preferred_element_type=F32)
            + jnp.dot(left[1][...], high, preferred_element_type=F32)
        )


def halves(ref):
    n = ref.shape[0]
    return ref[:, 0:n], ref[:, n : 2 * n]


def inverse_diagonal(real, imag):
    n = real.shape[-1]
    rows, columns = [], []
    on = lax.broadcasted_iota(jnp.int32, (128, 128), 0) == lax.broadcasted_iota(
        jnp.int32, (128, 128), 1
    )
    for at in range(0, n, 128):
        s = slice(at, at + 128)
        tiles = [jnp.where(on, part[s, s], 0.0) for part in (real, imag)]
        columns.append([jnp.sum(t, axis=1, keepdims=True) for t in tiles])
        rows.append([jnp.sum(t, axis=0, keepdims=True) for t in tiles])
    result = []
    for pieces, axis in ((rows, 1), (columns, 0)):
        dr = jnp.concatenate([p[0] for p in pieces], axis=axis)
        di = jnp.concatenate([p[1] for p in pieces], axis=axis)
        modulus = dr * dr + di * di
        result += [dr / modulus, -di / modulus]
    return result


def refined_inverse(real, imag, left, first, second, out):
    n = real.shape[-1]
    rows = slice(0, n)
    row_real, row_imag, col_real, col_imag = inverse_diagonal(real, imag)
    eye = (
        lax.broadcasted_iota(jnp.int32, (n, n), 0) == lax.broadcasted_iota(jnp.int32, (n, n), 1)
    ).astype(F32)
    m_real = real * row_real - imag * row_imag - eye
    m_imag = real * row_imag + imag * row_real
    put_left(left, rows, m_real, m_imag)
    put_right(first, m_real, m_imag)
    product(out, left, first)
    t_real, t_imag = halves(out)
    put_right(second, t_real, t_imag)
    q_real = eye - m_real + t_real
    q_imag = t_imag - m_imag
    product(out, left, second)
    s_real, s_imag = halves(out)
    q_real = q_real - s_real
    q_imag = q_imag - s_imag
    return col_real * q_real - col_imag * q_imag, col_real * q_imag + col_imag * q_real


def parity():
    return lax.axis_index("layer") % 2


def sandwich(which, coupling, even, inverse, left, result, scratch):
    lefts, others, first, second = scratch
    n = even.shape[-1]
    rows = slice(0, n)
    is_even = which == 0
    real, imag = coupling[0], coupling[1]
    real_t, imag_t = real.T, -imag.T
    put_left(lefts, rows, jnp.where(is_even, real, real_t), jnp.where(is_even, imag, imag_t))
    put_right(second, jnp.where(is_even, real_t, real), jnp.where(is_even, imag_t, imag))
    put_right(first, *inverse)
    product(left, lefts, first)
    put_left(others, rows, *halves(left))
    product(result, others, second)
    for part in range(2):
        columns = slice(part * n, (part + 1) * n)
        term = result[:, columns]
        result[:, columns] = jnp.where(is_even, even[part] - term, term)


def first_kernel(diag, couplings, inverse, left, result, odd, even, coupling, sems, *scratch):
    n = odd.shape[-1]
    which = parity()
    copies = [
        pltpu.make_async_copy(diag.at[0, 1, 0, 0], odd.at[0], sems.at[0]),
        pltpu.make_async_copy(diag.at[0, 1, 0, 1], odd.at[1], sems.at[1]),
        pltpu.make_async_copy(couplings.at[0, which], coupling, sems.at[2]),
        pltpu.make_async_copy(diag.at[0, 0, 0], even, sems.at[3]),
    ]
    for copy in copies:
        copy.start()
    copies[0].wait()
    copies[1].wait()
    pairs = [(scratch[i], scratch[i + 1]) for i in range(0, 8, 2)]
    lefts, others, first, second = pairs
    value = refined_inverse(odd[0], odd[1], lefts, first, second, result)
    inverse[:, 0:n] = value[0]
    inverse[:, n : 2 * n] = value[1]
    copies[2].wait()
    copies[3].wait()
    sandwich(which, coupling, even, value, left, result, pairs)


def second_kernel(diag, couplings, inverse, left, result, even, coupling, sems, *scratch):
    which = 1 - parity()
    copies = [
        pltpu.make_async_copy(couplings.at[0, which], coupling, sems.at[0]),
        pltpu.make_async_copy(diag.at[0, 0, 0], even, sems.at[1]),
    ]
    for copy in copies:
        copy.start()
    for copy in copies:
        copy.wait()
    pairs = [(scratch[i], scratch[i + 1]) for i in range(0, 8, 2)]
    sandwich(which, coupling, even, halves(inverse), left, result, pairs)


def cross_kernel(couplings, slow, fast, one, two, coupling, sems, *scratch):
    n = slow.shape[0]
    rows = slice(0, n)
    is_even = parity() == 0
    copy = pltpu.make_async_copy(couplings.at[0], coupling, sems.at[0])
    copy.start()
    lefts, others, first, second = [(scratch[i], scratch[i + 1]) for i in range(0, 8, 2)]
    put_left(lefts, rows, *[-v for v in halves(slow)])
    put_left(others, rows, *[-v for v in halves(fast)])
    copy.wait()
    even_right = (coupling[0, 0].T, -coupling[0, 1].T)
    odd_right = (coupling[1, 0], coupling[1, 1])
    put_right(first, *[jnp.where(is_even, o, e) for e, o in zip(even_right, odd_right)])
    put_right(second, *[jnp.where(is_even, e, o) for e, o in zip(even_right, odd_right)])
    product(one, lefts, first)
    product(two, others, second)


def reduced_term(start, real, imag, before, after, reduced, term, scratch):
    lefts, others, first, second = scratch
    n = real.shape[-1]
    rows = slice(0, n)
    value = refined_inverse(real, imag, lefts, first, second, term)
    put_left(others, rows, *halves(before))
    put_right(first, *value)
    product(term, others, first)
    put_left(lefts, rows, *halves(term))
    put_right(second, *halves(after))
    product(term, lefts, second)


def chip_kernel(mine, other, one, two, reduced, term, *scratch):
    n = mine.shape[0]
    is_even = parity() == 0
    parts = []
    for part, (a, b) in enumerate(zip(halves(mine), halves(other))):
        value = jnp.where(is_even, b - a, a - b)
        reduced[:, part * n : (part + 1) * n] = value
        parts.append(value)
    pairs = [(scratch[i], scratch[i + 1]) for i in range(0, 8, 2)]
    reduced_term(is_even, *parts, one, two, reduced, term, pairs)


def border_kernel(mine, other, one, two, reduced, chip_term, partial, term, *scratch):
    n = mine.shape[0]
    index = lax.axis_index("layer")
    is_even = index % 2 == 0
    is_last = index == lax.axis_size("layer") - 1
    parts = []
    for a, b in zip(halves(mine), halves(other)):
        parts.append(jnp.where(is_even, a - b, b - a))
    pairs = [(scratch[i], scratch[i + 1]) for i in range(0, 8, 2)]
    reduced_term(is_even, *parts, two, one, reduced, term, pairs)
    for part in range(2):
        columns = slice(part * n, (part + 1) * n)
        value = jnp.where(is_last, 0.0, term[:, columns])
        term[:, columns] = value
        partial[:, columns] = jnp.where(is_even, parts[part], reduced[:, columns]) - jnp.where(
            is_even, chip_term[:, columns], value
        )


def subtract_kernel(partial, border_term, rest, *scratch):
    rest[...] = partial[...] - border_term[...]


def greens_kernel(rest, chip_term, greens, *scratch):
    lefts, others, first, second = [(scratch[i], scratch[i + 1]) for i in range(0, 8, 2)]
    real, imag = [a - b for a, b in zip(halves(rest), halves(chip_term))]
    real, imag = refined_inverse(real, imag, lefts, first, second, scratch[8])
    greens[0] = real
    greens[1] = imag


def mix_kernel(phonon, strength, transfer, offset, blocks, mixed):
    energies, momenta, depth, width = blocks.shape
    stay, move = [], []
    for q in range(momenta):
        mode = transfer[q]
        weight = strength[mode]
        still = offset[mode] == 0
        stay.append(jnp.where(still, 2.0 * weight, 0.0))
        move.append(jnp.where(still, 0.0, weight))
    fold = [[phonon[e, f] for f in range(energies)] for e in range(energies)]
    for at in range(0, width, 128):
        columns = slice(at, at + 128)

        def rows_of(i, carry):
            rows = pl.ds(pl.multiple_of(i * 8, 8), 8)
            folded = []
            for k in range(momenta):
                g = [blocks[f, k, rows, columns] for f in range(energies)]
                folded.append(
                    [sum(fold[e][f] * g[f] for f in range(energies)) for e in range(energies)]
                )
            for k in range(momenta):
                moved = [
                    sum(move[q] * folded[(k - q) % momenta][e] for q in range(momenta))
                    for e in range(energies)
                ]
                for e in range(energies):
                    total = sum(stay[q] * folded[(k - q) % momenta][e] for q in range(momenta))
                    if e > 0:
                        total = total + moved[e - 1]
                    if e + 1 < energies:
                        total = total + moved[e + 1]
                    mixed[e, k, rows, columns] = total
            return carry

        lax.fori_loop(0, depth // 8, rows_of, 0)


def call(kernel, outs, operands, products, extra=(), sems=0):
    n = operands[0].shape[-2]

    def spec(shape):
        if len(shape) > 2 and shape[-1] == shape[-2]:
            return pl.BlockSpec(memory_space=pl.ANY)
        return pl.BlockSpec(shape, lambda i: (0,) * len(shape))

    scratch = [pltpu.VMEM(s, F32) for s in extra]
    if sems:
        scratch.append(pltpu.SemaphoreType.DMA((sems,)))
    scratch += [pltpu.VMEM((n, 2 * n), BF16)] * 4 + [pltpu.VMEM((2 * n, 2 * n), BF16)] * 4
    if kernel is subtract_kernel:
        scratch = []
    if kernel is greens_kernel:
        scratch.append(pltpu.VMEM((n, 2 * n), F32))
    return pl.pallas_call(
        kernel,
        out_shape=[jax.ShapeDtypeStruct(s, F32) for s in outs],
        grid=(1,),
        in_specs=[spec(o.shape) for o in operands],
        out_specs=[pl.BlockSpec(s, lambda i, r=len(s): (0,) * r) for s in outs],
        scratch_shapes=scratch,
        compiler_params=pltpu.CompilerParams(vmem_limit_bytes=28 * 1024 * 1024),
        cost_estimate=pl.CostEstimate(
            flops=3 * 10**10,
            bytes_accessed=1,
            transcendentals=0,
        ),
    )(*operands)


def swap(block, axis, first):
    route = []
    for i in range(first, lax.axis_size(axis) - 1, 2):
        route += [(i, i + 1), (i + 1, i)]
    return lax.ppermute(block, axis, route)


def ahead(block, axis, first):
    return lax.ppermute(
        block, axis, [(i, i + 1) for i in range(first, lax.axis_size(axis) - 1, 2)]
    )


def body(diag_blocks, couplings, phonon_matrix, mode_strength, transfer_mode, energy_offset):
    n = diag_blocks.shape[-1]
    wide, square = (n, 2 * n), (2, n, n)

    def whole(shape):
        return pl.BlockSpec(shape, lambda i: (0,) * len(shape))

    diag_blocks, couplings = [
        pltpu.with_memory_space_constraint(v, pltpu.HBM) for v in (diag_blocks, couplings)
    ]
    inverse, slow, border = call(
        first_kernel, [wide] * 3, (diag_blocks, couplings), 4, [square] * 3, 4
    )
    border_other = swap(border, "layer", 1)
    fast, chip = call(
        second_kernel, [wide] * 2, (diag_blocks, couplings, inverse), 2, [square] * 2, 2
    )
    chip_other = swap(chip, "layer", 0)
    one, two = call(cross_kernel, [wide] * 2, (couplings, slow, fast), 2, [(2,) + square], 1)
    reduced, chip_term = call(chip_kernel, [wide] * 2, (chip, chip_other, one, two), 4)
    from_border = ahead(chip_term, "layer", 1)
    partial, border_term = call(
        border_kernel, [wide] * 2, (border, border_other, one, two, reduced, chip_term), 4
    )
    from_chip = ahead(border_term, "layer", 0)
    (rest,) = call(subtract_kernel, [wide], (partial, from_border), 0)
    (greens,) = call(greens_kernel, [square], (rest, from_chip), 2)
    energies, momenta = lax.axis_size("energy"), lax.axis_size("momentum")
    group = energies * momenta
    depth = 2 * n // group
    axes = ("energy", "momentum")
    spread = lax.all_to_all(
        greens.reshape(group, depth, n), axes, split_axis=0, concat_axis=0, tiled=True
    )
    block = (energies, momenta, depth, n)
    small = pl.BlockSpec(memory_space=pltpu.SMEM)
    mixed = pl.pallas_call(
        mix_kernel,
        out_shape=jax.ShapeDtypeStruct(block, F32),
        grid=(1,),
        in_specs=[small] * 4 + [whole(block)],
        out_specs=whole(block),
        compiler_params=pltpu.CompilerParams(vmem_limit_bytes=12 * 1024 * 1024),
    )(phonon_matrix, mode_strength, transfer_mode, energy_offset, spread.reshape(block))
    returned = lax.all_to_all(
        mixed.reshape(group, depth, n), axes, split_axis=0, concat_axis=0, tiled=True
    )
    return returned.reshape(1, 1, 1, 2, n, n)


def solution(mesh):
    return jax.shard_map(
        body,
        mesh=mesh,
        in_specs=(
            P("momentum", "layer", "energy", None, None, None),
            P("momentum", "layer", None, None, None),
            P(),
            P(),
            P(),
            P(),
        ),
        out_specs=P("momentum", "layer", "energy", None, None, None),
        check_vma=False,
    )
```

```python
import jax
import jax.numpy as jnp
from jax import lax
from jax.experimental import pallas as pl
from jax.experimental.pallas import tpu as pltpu
from jax.sharding import PartitionSpec as P

F32 = jnp.float32
BF16 = jnp.bfloat16


def split(value):
    high = value.astype(BF16)
    return high, (value - high.astype(F32)).astype(BF16)


LANES = 128


def cut(at):
    return slice(LANES * at, LANES * (at + 1))


def pair(at):
    return slice(2 * LANES * at, 2 * LANES * (at + 1))


def real_of(at):
    return slice(2 * LANES * at, 2 * LANES * at + LANES)


def imag_of(at):
    return slice(2 * LANES * at + LANES, 2 * LANES * (at + 1))


def put_left(left, at, real, imag):
    for columns, part in ((real_of(at), real), (imag_of(at), imag)):
        for ref, value in zip(left, split(part)):
            ref[:, columns] = value


def put_right(right, at, real, imag):
    for ref, r, i in zip(right, split(real), split(imag)):
        minus = -i
        for k in range(real.shape[0] // LANES):
            rows = cut(k)
            ref[real_of(k), real_of(at)] = r[rows]
            ref[real_of(k), imag_of(at)] = i[rows]
            ref[imag_of(k), real_of(at)] = minus[rows]
            ref[imag_of(k), imag_of(at)] = r[rows]


def product(left, right, epilogue, fill=()):
    for at in range(right[0].shape[1] // (2 * LANES)):
        columns = pair(at)
        high = right[0][:, columns]
        lh = left[0][...]
        value = (
            jnp.dot(lh, high, preferred_element_type=F32)
            + jnp.dot(lh, right[1][:, columns], preferred_element_type=F32)
            + jnp.dot(left[1][...], high, preferred_element_type=F32)
        )
        if at < len(fill):
            fill[at]()
        epilogue(at, value[:, :LANES], value[:, LANES:])


def storing(out):
    def epilogue(at, real, imag):
        out[:, real_of(at)] = real
        out[:, imag_of(at)] = imag

    return epilogue


def wide_chunk(ref, at):
    return ref[:, real_of(at)], ref[:, imag_of(at)]


def refined_inverse(chunk, left, first, second, rest, epilogue, fill=(), more=()):
    n = rest.shape[0]
    count = n // LANES
    on = lax.broadcasted_iota(jnp.int32, (LANES, LANES), 0) == lax.broadcasted_iota(
        jnp.int32, (LANES, LANES), 1
    )
    eye = on.astype(F32)
    column_parts = []
    for at in range(count):
        real, imag = chunk(at)
        tiles = [jnp.where(on, part[cut(at)], 0.0) for part in (real, imag)]
        pieces = []
        for axis in (0, 1):
            dr, di = [jnp.sum(t, axis=axis, keepdims=True) for t in tiles]
            modulus = dr * dr + di * di
            pieces.append((dr / modulus, -di / modulus))
        (xr, xi), column = pieces
        column_parts.append(column)
        m_real = real * xr - imag * xi
        m_imag = real * xi + imag * xr
        m_real = jnp.concatenate(
            [m_real[cut(k)] - eye if k == at else m_real[cut(k)] for k in range(count)], axis=0
        )
        put_left(left, at, m_real, m_imag)
        put_right(first, at, m_real, m_imag)
        rest[:, real_of(at)] = -m_real
        rest[:, imag_of(at)] = -m_imag

    def square(at, real, imag):
        put_right(second, at, real, imag)
        rest[:, real_of(at)] += real
        rest[:, imag_of(at)] += imag
        rest[cut(at), real_of(at)] += eye

    product(left, first, square, fill)
    col_real, col_imag = [
        jnp.concatenate([c[part] for c in column_parts], axis=0) for part in range(2)
    ]

    def finish(at, real, imag):
        q_real = rest[:, real_of(at)] - real
        q_imag = rest[:, imag_of(at)] - imag
        epilogue(at, col_real * q_real - col_imag * q_imag, col_real * q_imag + col_imag * q_real)

    product(left, second, finish, more)


def pairs_of(refs):
    return [(refs[i], refs[i + 1]) for i in range(0, len(refs), 2)]


def parity():
    return lax.axis_index("layer") % 2


def factors(which, coupling, left, right):
    is_even = which == 0

    def fill(at):
        def run():
            real, imag = coupling[0, :, cut(at)], coupling[1, :, cut(at)]
            real_t, imag_t = coupling[0, cut(at), :].T, -coupling[1, cut(at), :].T
            put_left(left, at, jnp.where(is_even, real, real_t), jnp.where(is_even, imag, imag_t))
            put_right(
                right, at, jnp.where(is_even, real_t, real), jnp.where(is_even, imag_t, imag)
            )

        return run

    return [fill(at) for at in range(coupling.shape[-1] // LANES)]


def sandwich(which, even, left, inverse, right, half, result):
    is_even = which == 0
    product(left, inverse, lambda at, real, imag: put_left(half, at, real, imag))

    def finish(at, real, imag):
        for part, (columns, term) in enumerate(((real_of(at), real), (imag_of(at), imag))):
            result[:, columns] = jnp.where(is_even, even[part, :, cut(at)] - term, term)

    product(half, right, finish)


def first_kernel(diag, couplings, *refs):
    inverse, right, half, far_left, far_right = pairs_of(refs[:10])
    even, border, odd, near, far, sems = refs[10:16]
    left, other, first, second = pairs_of(refs[16:24])
    rest = refs[24]
    which = parity()
    count = odd.shape[-1] // LANES
    urgent = [
        pltpu.make_async_copy(diag.at[0, 1, 0, :, :, cut(at)], odd.at[:, :, cut(at)], sems.at[at])
        for at in range(count)
    ]
    later = [
        pltpu.make_async_copy(couplings.at[0, which], near, sems.at[count]),
        pltpu.make_async_copy(diag.at[0, 0, 0], even, sems.at[count + 1]),
        pltpu.make_async_copy(couplings.at[0, 1 - which], far, sems.at[count + 2]),
    ]
    for copy in urgent:
        copy.start()

    def chunk(at):
        urgent[at].wait()
        if at == count - 1:
            for copy in later:
                copy.start()
        return odd[0, :, cut(at)], odd[1, :, cut(at)]

    def after(copy, runs):
        def start():
            copy.wait()
            runs[0]()

        return [start] + runs[1:]

    refined_inverse(
        chunk,
        left,
        first,
        second,
        rest,
        lambda at, real, imag: put_right(inverse, at, real, imag),
        after(later[0], factors(which, near, other, right)),
        after(later[2], factors(1 - which, far, far_left, far_right)),
    )
    later[1].wait()
    sandwich(which, even, other, inverse, right, half, border)


def second_kernel(even, *refs):
    inverse, left, right, half = pairs_of(refs[:8])
    sandwich(1 - parity(), even, left, inverse, right, half, refs[8])


def cross_kernel(*refs):
    slow, slow_right, fast, fast_right = pairs_of(refs[:8])
    one, two = refs[8:]
    product(slow, fast_right, lambda at, real, imag: storing(one)(at, -real, -imag))
    product(fast, slow_right, lambda at, real, imag: storing(two)(at, -real, -imag))


def reduced_term(chunk, before, after, rest, epilogue, scratch):
    left, other, first, second, third = scratch
    count = before.shape[0] // LANES
    refined_inverse(
        chunk,
        left,
        first,
        second,
        rest,
        lambda at, real, imag: put_right(first, at, real, imag),
        [lambda at=at: put_left(other, at, *wide_chunk(before, at)) for at in range(count)],
        [lambda at=at: put_right(third, at, *wide_chunk(after, at)) for at in range(count)],
    )
    product(other, first, lambda at, real, imag: put_left(left, at, real, imag))
    product(left, third, epilogue)


def chip_kernel(mine, far, one, two, reduced, term, *refs):
    is_even = parity() == 0

    def chunk(at):
        parts = [
            jnp.where(is_even, b - a, a - b)
            for a, b in zip(wide_chunk(mine, at), wide_chunk(far, at))
        ]
        storing(reduced)(at, *parts)
        return parts

    reduced_term(chunk, one, two, refs[0], storing(term), pairs_of(refs[1:]))


def border_kernel(mine, far, one, two, reduced, chip_term, partial, term, *refs):
    index = lax.axis_index("layer")
    is_even = index % 2 == 0
    is_last = index == lax.axis_size("layer") - 1

    def chunk(at):
        parts = [
            jnp.where(is_even, a - b, b - a)
            for a, b in zip(wide_chunk(mine, at), wide_chunk(far, at))
        ]
        for columns, value in zip((real_of(at), imag_of(at)), parts):
            partial[:, columns] = jnp.where(
                is_even, value - chip_term[:, columns], reduced[:, columns]
            )
        return parts

    def finish(at, real, imag):
        for columns, value in ((real_of(at), real), (imag_of(at), imag)):
            value = jnp.where(is_last, 0.0, value)
            term[:, columns] = value
            partial[:, columns] -= jnp.where(is_even, 0.0, value)

    reduced_term(chunk, two, one, refs[0], finish, pairs_of(refs[1:]))


def greens_of(chunk, greens, refs):
    left, first, second = pairs_of(refs[1:])

    def finish(at, real, imag):
        greens[0, :, cut(at)] = real
        greens[1, :, cut(at)] = imag

    refined_inverse(chunk, left, first, second, refs[0], finish)


def weights_kernel(strength, transfer, offset, weights):
    for q in range(weights.shape[1]):
        mode = transfer[q]
        weight = strength[mode]
        still = offset[mode] == 0
        weights[0, q] = jnp.where(still, 2.0 * weight, 0.0)
        weights[1, q] = jnp.where(still, 0.0, weight)


def odd_greens_kernel(partial, chip_term, weights, greens, *refs):
    @pl.when(parity() == 1)
    def _():
        def chunk(at):
            return [a - b for a, b in zip(wide_chunk(partial, at), wide_chunk(chip_term, at))]

        greens_of(chunk, greens, refs)


def even_greens_kernel(partial, border_term, odd_greens, greens, *refs):
    @pl.when(parity() == 0)
    def _():
        def chunk(at):
            return [a - b for a, b in zip(wide_chunk(partial, at), wide_chunk(border_term, at))]

        greens_of(chunk, greens, refs)


def mix_kernel(phonon, weights, blocks, mixed):
    energies, momenta, depth, width = blocks.shape
    stay, move = [[weights[row, q] for q in range(momenta)] for row in range(2)]
    fold = [[phonon[e, f] for f in range(energies)] for e in range(energies)]
    for at in range(0, width, 128):
        columns = slice(at, at + 128)

        def rows_of(i, carry):
            rows = pl.ds(pl.multiple_of(i * 8, 8), 8)
            folded = []
            for k in range(momenta):
                g = [blocks[f, k, rows, columns] for f in range(energies)]
                folded.append(
                    [sum(fold[e][f] * g[f] for f in range(energies)) for e in range(energies)]
                )
            for k in range(momenta):
                moved = [
                    sum(move[q] * folded[(k - q) % momenta][e] for q in range(momenta))
                    for e in range(energies)
                ]
                for e in range(energies):
                    total = sum(stay[q] * folded[(k - q) % momenta][e] for q in range(momenta))
                    if e > 0:
                        total = total + moved[e - 1]
                    if e + 1 < energies:
                        total = total + moved[e + 1]
                    mixed[e, k, rows, columns] = total
            return carry

        lax.fori_loop(0, depth // 8, rows_of, 0)


def call(kernel, outs, operands, scratch=(), aliases=()):
    def spec(value):
        if value.ndim > 3:
            return pl.BlockSpec(memory_space=pl.ANY)
        if value.shape[-1] < LANES:
            return pl.BlockSpec(memory_space=pltpu.SMEM)
        return pl.BlockSpec(memory_space=pltpu.VMEM)

    return pl.pallas_call(
        kernel,
        out_shape=outs,
        in_specs=[spec(o) for o in operands],
        out_specs=[spec(o) for o in outs],
        scratch_shapes=list(scratch),
        input_output_aliases=dict(aliases),
        compiler_params=pltpu.CompilerParams(vmem_limit_bytes=20 * 1024 * 1024),
        cost_estimate=pl.CostEstimate(flops=COST[kernel.__name__], bytes_accessed=1, transcendentals=0),
    )(*operands)


def swap(block, axis, first):
    route = []
    for i in range(first, lax.axis_size(axis) - 1, 2):
        route += [(i, i + 1), (i + 1, i)]
    return lax.ppermute(block, axis, route)


def ahead(block, axis, first):
    return lax.ppermute(
        block, axis, [(i, i + 1) for i in range(first, lax.axis_size(axis) - 1, 2)]
    )


def body(diag_blocks, couplings, phonon_matrix, mode_strength, transfer_mode, energy_offset):
    n = diag_blocks.shape[-1]
    wide = jax.ShapeDtypeStruct((n, 2 * n), F32)
    square = jax.ShapeDtypeStruct((2, n, n), F32)
    left = [jax.ShapeDtypeStruct((n, 2 * n), BF16)] * 2
    right = [jax.ShapeDtypeStruct((2 * n, 2 * n), BF16)] * 2
    flat = [pltpu.VMEM((n, 2 * n), F32)]
    block = [pltpu.VMEM((2, n, n), F32)]
    lefts = [pltpu.VMEM((n, 2 * n), BF16)] * 2
    rights = [pltpu.VMEM((2 * n, 2 * n), BF16)] * 2

    def whole(shape):
        return pl.BlockSpec(shape, lambda i: (0,) * len(shape))

    diag_blocks, couplings = [
        pltpu.with_memory_space_constraint(v, pltpu.HBM) for v in (diag_blocks, couplings)
    ]
    *parts, even, border = call(
        first_kernel,
        right + right + left + left + right + [square, wide],
        (diag_blocks, couplings),
        block * 3 + [pltpu.SemaphoreType.DMA((n // LANES + 3,))] + lefts * 2 + rights * 2 + flat,
    )
    inverse, slow_right, slow, fast_left, fast_right = [parts[i : i + 2] for i in range(0, 10, 2)]
    border_far = swap(border, "layer", 1)
    *fast, chip = call(
        second_kernel, left + [wide], (even, *inverse, *fast_left, *fast_right)
    )
    chip, border = lax.optimization_barrier((chip, border))
    chip_far = swap(chip, "layer", 0)
    one, two = call(cross_kernel, [wide] * 2, (*slow, *slow_right, *fast, *fast_right))
    scratch = flat + lefts * 2 + rights * 3
    reduced, chip_term = call(chip_kernel, [wide] * 2, (chip, chip_far, one, two), scratch)
    from_border = ahead(chip_term, "layer", 1)
    partial, border_term = call(
        border_kernel, [wide] * 2, (border, border_far, one, two, reduced, chip_term), scratch
    )
    from_chip = ahead(border_term, "layer", 0)
    scratch = flat + lefts + rights * 2
    small = pl.BlockSpec(memory_space=pltpu.SMEM)
    transfers = jax.ShapeDtypeStruct((2,) + transfer_mode.shape, F32)
    (weights,) = call(
        weights_kernel, [transfers], (mode_strength, transfer_mode, energy_offset)
    )
    (greens,) = call(odd_greens_kernel, [square], (partial, from_chip, weights), scratch)
    (greens,) = call(
        even_greens_kernel, [square], (partial, from_border, greens), scratch, aliases={2: 0}
    )
    energies, momenta = lax.axis_size("energy"), lax.axis_size("momentum")
    group = energies * momenta
    depth = 2 * n // group
    axes = ("energy", "momentum")
    spread = lax.all_to_all(
        greens.reshape(group, depth, n), axes, split_axis=0, concat_axis=0, tiled=True
    )
    block = (energies, momenta, depth, n)
    mixed = pl.pallas_call(
        mix_kernel,
        out_shape=jax.ShapeDtypeStruct(block, F32),
        grid=(1,),
        in_specs=[small] * 2 + [whole(block)],
        out_specs=whole(block),
        compiler_params=pltpu.CompilerParams(vmem_limit_bytes=12 * 1024 * 1024),
    )(phonon_matrix, weights, spread.reshape(block))
    returned = lax.all_to_all(
        mixed.reshape(group, depth, n), axes, split_axis=0, concat_axis=0, tiled=True
    )
    return returned.reshape(1, 1, 1, 2, n, n)


COST = dict(weights_kernel=3 * 10**10, first_kernel=3 * 10**10, second_kernel=3 * 10**10, cross_kernel=3 * 10**10, chip_kernel=3 * 10**10, border_kernel=3 * 10**10, odd_greens_kernel=1, even_greens_kernel=3 * 10**10)


def solution(mesh):
    return jax.shard_map(
        body,
        mesh=mesh,
        in_specs=(
            P("momentum", "layer", "energy", None, None, None),
            P("momentum", "layer", None, None, None),
            P(),
            P(),
            P(),
            P(),
        ),
        out_specs=P("momentum", "layer", "energy", None, None, None),
        check_vma=False,
    )
```

```python
import jax
import jax.numpy as jnp
from jax import lax
from jax.experimental import pallas as pl
from jax.experimental.pallas import tpu as pltpu
from jax.sharding import PartitionSpec as P

F32 = jnp.float32
BF16 = jnp.bfloat16


def split(value):
    high = value.astype(BF16)
    return high, (value - high.astype(F32)).astype(BF16)


LANES = 128


def cut(at):
    return slice(LANES * at, LANES * (at + 1))


def pair(at):
    return slice(2 * LANES * at, 2 * LANES * (at + 1))


def real_of(at):
    return slice(2 * LANES * at, 2 * LANES * at + LANES)


def imag_of(at):
    return slice(2 * LANES * at + LANES, 2 * LANES * (at + 1))


def put_left(left, at, real, imag):
    for columns, part in ((real_of(at), real), (imag_of(at), imag)):
        for ref, value in zip(left, split(part)):
            ref[:, columns] = value


def put_right(right, at, real, imag):
    for ref, r, i in zip(right, split(real), split(imag)):
        minus = -i
        for k in range(real.shape[0] // LANES):
            rows = cut(k)
            ref[real_of(k), real_of(at)] = r[rows]
            ref[real_of(k), imag_of(at)] = i[rows]
            ref[imag_of(k), real_of(at)] = minus[rows]
            ref[imag_of(k), imag_of(at)] = r[rows]


def product(left, right, epilogue, fill=()):
    for at in range(right[0].shape[1] // (2 * LANES)):
        columns = pair(at)
        high = right[0][:, columns]
        lh = left[0][...]
        value = jnp.dot(lh, high, preferred_element_type=F32)
        for low in right[1:]:
            value += jnp.dot(lh, low[:, columns], preferred_element_type=F32)
        for low in left[1:]:
            value += jnp.dot(low[...], high, preferred_element_type=F32)
        if at < len(fill):
            fill[at]()
        epilogue(at, value[:, :LANES], value[:, LANES:])


def storing(out):
    def epilogue(at, real, imag):
        out[:, real_of(at)] = real
        out[:, imag_of(at)] = imag

    return epilogue


def wide_chunk(ref, at):
    return ref[:, real_of(at)], ref[:, imag_of(at)]


def refined_inverse(chunk, left, first, second, rest, epilogue, fill=(), more=()):
    n = rest.shape[0]
    count = n // LANES
    on = lax.broadcasted_iota(jnp.int32, (LANES, LANES), 0) == lax.broadcasted_iota(
        jnp.int32, (LANES, LANES), 1
    )
    eye = on.astype(F32)
    column_parts = []
    for at in range(count):
        real, imag = chunk(at)
        tiles = [jnp.where(on, part[cut(at)], 0.0) for part in (real, imag)]
        pieces = []
        for axis in (0, 1):
            dr, di = [jnp.sum(t, axis=axis, keepdims=True) for t in tiles]
            modulus = dr * dr + di * di
            pieces.append((dr / modulus, -di / modulus))
        (xr, xi), column = pieces
        column_parts.append(column)
        m_real = real * xr - imag * xi
        m_imag = real * xi + imag * xr
        m_real = jnp.concatenate(
            [m_real[cut(k)] - eye if k == at else m_real[cut(k)] for k in range(count)], axis=0
        )
        put_left(left, at, m_real, m_imag)
        put_right(first, at, m_real, m_imag)
        rest[:, real_of(at)] = -m_real
        rest[:, imag_of(at)] = -m_imag

    def square(at, real, imag):
        put_right(second, at, real, imag)
        rest[:, real_of(at)] += real
        rest[:, imag_of(at)] += imag
        rest[cut(at), real_of(at)] += eye

    product(left, first, square, fill)
    col_real, col_imag = [
        jnp.concatenate([c[part] for c in column_parts], axis=0) for part in range(2)
    ]

    def finish(at, real, imag):
        q_real = rest[:, real_of(at)] - real
        q_imag = rest[:, imag_of(at)] - imag
        epilogue(at, col_real * q_real - col_imag * q_imag, col_real * q_imag + col_imag * q_real)

    product(left, second, finish, more)


def pairs_of(refs):
    return [(refs[i], refs[i + 1]) for i in range(0, len(refs), 2)]


def parity():
    return lax.axis_index("layer") % 2


def factors(which, coupling, left, right):
    is_even = which == 0

    def fill(at):
        def run():
            real, imag = coupling[0, :, cut(at)], coupling[1, :, cut(at)]
            real_t, imag_t = coupling[0, cut(at), :].T, -coupling[1, cut(at), :].T
            put_left(left, at, jnp.where(is_even, real, real_t), jnp.where(is_even, imag, imag_t))
            put_right(
                right, at, jnp.where(is_even, real_t, real), jnp.where(is_even, imag_t, imag)
            )

        return run

    return [fill(at) for at in range(coupling.shape[-1] // LANES)]


def sandwich(which, even, left, inverse, right, half, result):
    is_even = which == 0
    product(left, inverse, lambda at, real, imag: put_left(half, at, real, imag))

    def finish(at, real, imag):
        for part, (columns, term) in enumerate(((real_of(at), real), (imag_of(at), imag))):
            result[:, columns] = jnp.where(is_even, even[part, :, cut(at)] - term, term)

    product(half, right, finish)


def first_kernel(diag, couplings, *refs):
    inverse, right, half, far_left, far_right = pairs_of(refs[:10])
    even, border, odd, near, far, sems = refs[10:16]
    left, other, first, second = pairs_of(refs[16:24])
    rest = refs[24]
    which = parity()
    count = odd.shape[-1] // LANES
    urgent = [
        pltpu.make_async_copy(
            diag.at[0, 1, 0, part, cut(at)], odd.at[part, cut(at)], sems.at[part * count + at]
        )
        for part in range(2)
        for at in range(count)
    ]
    later = [
        pltpu.make_async_copy(couplings.at[0, which], near, sems.at[2 * count]),
        pltpu.make_async_copy(diag.at[0, 0, 0], even, sems.at[2 * count + 1]),
        pltpu.make_async_copy(couplings.at[0, 1 - which], far, sems.at[2 * count + 2]),
    ]
    for copy in urgent:
        copy.start()

    for copy in urgent:
        copy.wait()
    for copy in later:
        copy.start()

    def chunk(at):
        return odd[0, :, cut(at)], odd[1, :, cut(at)]

    def after(copy, runs):
        def start():
            copy.wait()
            runs[0]()

        return [start] + runs[1:]

    refined_inverse(
        chunk,
        left[:1],
        first[:1],
        second[:1],
        rest,
        lambda at, real, imag: put_right(inverse, at, real, imag),
        after(later[0], factors(which, near, other, right)),
        after(later[2], factors(1 - which, far, far_left, far_right)),
    )
    later[1].wait()
    sandwich(which, even, other, inverse, right, half, border)


def second_kernel(even, *refs):
    inverse, left, right, half = pairs_of(refs[:8])
    sandwich(1 - parity(), even, left, inverse, right, half, refs[8])


def cross_kernel(*refs):
    slow, slow_right, fast, fast_right = pairs_of(refs[:8])
    one, two = refs[8:]
    product(slow, fast_right, lambda at, real, imag: storing(one)(at, -real, -imag))
    product(fast, slow_right, lambda at, real, imag: storing(two)(at, -real, -imag))


def reduced_term(chunk, before, after, rest, epilogue, scratch):
    left, other, first, second, third = scratch
    count = before.shape[0] // LANES
    refined_inverse(
        chunk,
        left[:1],
        first[:1],
        second[:1],
        rest,
        lambda at, real, imag: put_right(first, at, real, imag),
        [lambda at=at: put_left(other, at, *wide_chunk(before, at)) for at in range(count)],
        [lambda at=at: put_right(third, at, *wide_chunk(after, at)) for at in range(count)],
    )
    product(other, first, lambda at, real, imag: put_left(left, at, real, imag))
    product(left, third, epilogue)


def chip_kernel(mine, far, one, two, reduced, term, *refs):
    is_even = parity() == 0

    def chunk(at):
        parts = [
            jnp.where(is_even, b - a, a - b)
            for a, b in zip(wide_chunk(mine, at), wide_chunk(far, at))
        ]
        storing(reduced)(at, *parts)
        return parts

    reduced_term(chunk, one, two, refs[0], storing(term), pairs_of(refs[1:]))


def border_kernel(mine, far, one, two, reduced, chip_term, partial, term, *refs):
    index = lax.axis_index("layer")
    is_even = index % 2 == 0
    is_last = index == lax.axis_size("layer") - 1

    def chunk(at):
        parts = [
            jnp.where(is_even, a - b, b - a)
            for a, b in zip(wide_chunk(mine, at), wide_chunk(far, at))
        ]
        for columns, value in zip((real_of(at), imag_of(at)), parts):
            partial[:, columns] = jnp.where(
                is_even, value - chip_term[:, columns], reduced[:, columns]
            )
        return parts

    def finish(at, real, imag):
        for columns, value in ((real_of(at), real), (imag_of(at), imag)):
            value = jnp.where(is_last, 0.0, value)
            term[:, columns] = value
            partial[:, columns] -= jnp.where(is_even, 0.0, value)

    reduced_term(chunk, two, one, refs[0], finish, pairs_of(refs[1:]))


def greens_of(chunk, greens, refs):
    left, first, second = pairs_of(refs[1:])

    def finish(at, real, imag):
        greens[0, :, cut(at)] = real
        greens[1, :, cut(at)] = imag

    refined_inverse(chunk, left, first, second, refs[0], finish)


def weights_kernel(strength, transfer, offset, weights):
    for q in range(weights.shape[1]):
        mode = transfer[q]
        weight = strength[mode]
        still = offset[mode] == 0
        weights[0, q] = jnp.where(still, 2.0 * weight, 0.0)
        weights[1, q] = jnp.where(still, 0.0, weight)


def odd_greens_kernel(partial, chip_term, weights, greens, *refs):
    @pl.when(parity() == 1)
    def _():
        def chunk(at):
            return [a - b for a, b in zip(wide_chunk(partial, at), wide_chunk(chip_term, at))]

        greens_of(chunk, greens, refs)


def even_greens_kernel(partial, border_term, odd_greens, greens, *refs):
    @pl.when(parity() == 0)
    def _():
        def chunk(at):
            return [a - b for a, b in zip(wide_chunk(partial, at), wide_chunk(border_term, at))]

        greens_of(chunk, greens, refs)


def mix_kernel(phonon, weights, blocks, mixed):
    energies, momenta, depth, width = blocks.shape
    stay, move = [[weights[row, q] for q in range(momenta)] for row in range(2)]
    fold = [[phonon[e, f] for f in range(energies)] for e in range(energies)]
    for at in range(0, width, 128):
        columns = slice(at, at + 128)

        def rows_of(i, carry):
            rows = pl.ds(pl.multiple_of(i * 8, 8), 8)
            folded = []
            for k in range(momenta):
                g = [blocks[f, k, rows, columns] for f in range(energies)]
                folded.append(
                    [sum(fold[e][f] * g[f] for f in range(energies)) for e in range(energies)]
                )
            for k in range(momenta):
                moved = [
                    sum(move[q] * folded[(k - q) % momenta][e] for q in range(momenta))
                    for e in range(energies)
                ]
                for e in range(energies):
                    total = sum(stay[q] * folded[(k - q) % momenta][e] for q in range(momenta))
                    if e > 0:
                        total = total + moved[e - 1]
                    if e + 1 < energies:
                        total = total + moved[e + 1]
                    mixed[e, k, rows, columns] = total
            return carry

        lax.fori_loop(0, depth // 8, rows_of, 0)


def call(kernel, outs, operands, scratch=(), aliases=()):
    def spec(value):
        if value.ndim > 3:
            return pl.BlockSpec(memory_space=pl.ANY)
        if value.shape[-1] < LANES:
            return pl.BlockSpec(memory_space=pltpu.SMEM)
        return pl.BlockSpec(memory_space=pltpu.VMEM)

    return pl.pallas_call(
        kernel,
        out_shape=outs,
        in_specs=[spec(o) for o in operands],
        out_specs=[spec(o) for o in outs],
        scratch_shapes=list(scratch),
        input_output_aliases=dict(aliases),
        compiler_params=pltpu.CompilerParams(vmem_limit_bytes=20 * 1024 * 1024),
        cost_estimate=pl.CostEstimate(flops=COST[kernel.__name__], bytes_accessed=1, transcendentals=0),
    )(*operands)


def swap(block, axis, first):
    route = []
    for i in range(first, lax.axis_size(axis) - 1, 2):
        route += [(i, i + 1), (i + 1, i)]
    return lax.ppermute(block, axis, route)


def ahead(block, axis, first):
    return lax.ppermute(
        block, axis, [(i, i + 1) for i in range(first, lax.axis_size(axis) - 1, 2)]
    )


def body(diag_blocks, couplings, phonon_matrix, mode_strength, transfer_mode, energy_offset):
    n = diag_blocks.shape[-1]
    wide = jax.ShapeDtypeStruct((n, 2 * n), F32)
    square = jax.ShapeDtypeStruct((2, n, n), F32)
    left = [jax.ShapeDtypeStruct((n, 2 * n), BF16)] * 2
    right = [jax.ShapeDtypeStruct((2 * n, 2 * n), BF16)] * 2
    flat = [pltpu.VMEM((n, 2 * n), F32)]
    block = [pltpu.VMEM((2, n, n), F32)]
    lefts = [pltpu.VMEM((n, 2 * n), BF16)] * 2
    rights = [pltpu.VMEM((2 * n, 2 * n), BF16)] * 2

    def whole(shape):
        return pl.BlockSpec(shape, lambda i: (0,) * len(shape))

    diag_blocks, couplings = [
        pltpu.with_memory_space_constraint(v, pltpu.HBM) for v in (diag_blocks, couplings)
    ]
    *parts, even, border = call(
        first_kernel,
        right + right + left + left + right + [square, wide],
        (diag_blocks, couplings),
        block * 3 + [pltpu.SemaphoreType.DMA((2 * (n // LANES) + 3,))] + lefts * 2 + rights * 2 + flat,
    )
    inverse, slow_right, slow, fast_left, fast_right = [parts[i : i + 2] for i in range(0, 10, 2)]
    border_far = swap(border, "layer", 1)
    *fast, chip = call(
        second_kernel, left + [wide], (even, *inverse, *fast_left, *fast_right)
    )
    chip, border = lax.optimization_barrier((chip, border))
    chip_far = swap(chip, "layer", 0)
    one, two = call(cross_kernel, [wide] * 2, (*slow, *slow_right, *fast, *fast_right))
    scratch = flat + lefts * 2 + rights * 3
    reduced, chip_term = call(chip_kernel, [wide] * 2, (chip, chip_far, one, two), scratch)
    from_border = ahead(chip_term, "layer", 1)
    partial, border_term = call(
        border_kernel, [wide] * 2, (border, border_far, one, two, reduced, chip_term), scratch
    )
    from_chip = ahead(border_term, "layer", 0)
    scratch = flat + lefts + rights * 2
    small = pl.BlockSpec(memory_space=pltpu.SMEM)
    transfers = jax.ShapeDtypeStruct((2,) + transfer_mode.shape, F32)
    (weights,) = call(
        weights_kernel, [transfers], (mode_strength, transfer_mode, energy_offset)
    )
    (greens,) = call(odd_greens_kernel, [square], (partial, from_chip, weights), scratch)
    (greens,) = call(
        even_greens_kernel, [square], (partial, from_border, greens), scratch, aliases={2: 0}
    )
    energies, momenta = lax.axis_size("energy"), lax.axis_size("momentum")
    group = energies * momenta
    depth = 2 * n // group
    axes = ("energy", "momentum")
    spread = lax.all_to_all(
        greens.reshape(group, depth, n), axes, split_axis=0, concat_axis=0, tiled=True
    )
    block = (energies, momenta, depth, n)
    mixed = pl.pallas_call(
        mix_kernel,
        out_shape=jax.ShapeDtypeStruct(block, F32),
        grid=(1,),
        in_specs=[small] * 2 + [whole(block)],
        out_specs=whole(block),
        compiler_params=pltpu.CompilerParams(vmem_limit_bytes=12 * 1024 * 1024),
    )(phonon_matrix, weights, spread.reshape(block))
    returned = lax.all_to_all(
        mixed.reshape(group, depth, n), axes, split_axis=0, concat_axis=0, tiled=True
    )
    return returned.reshape(1, 1, 1, 2, n, n)


COST = dict(weights_kernel=3 * 10**10, first_kernel=3 * 10**10, second_kernel=3 * 10**10, cross_kernel=3 * 10**10, chip_kernel=3 * 10**10, border_kernel=3 * 10**10, odd_greens_kernel=1, even_greens_kernel=3 * 10**10)


def solution(mesh):
    return jax.shard_map(
        body,
        mesh=mesh,
        in_specs=(
            P("momentum", "layer", "energy", None, None, None),
            P("momentum", "layer", None, None, None),
            P(),
            P(),
            P(),
            P(),
        ),
        out_specs=P("momentum", "layer", "energy", None, None, None),
        check_vma=False,
    )
```

```python
import jax
import jax.numpy as jnp
from jax import lax
from jax.experimental import pallas as pl
from jax.experimental.pallas import tpu as pltpu
from jax.sharding import PartitionSpec as P

F32 = jnp.float32
BF16 = jnp.bfloat16


def split(value):
    high = value.astype(BF16)
    return high, (value - high.astype(F32)).astype(BF16)


LANES = 128


def cut(at):
    return slice(LANES * at, LANES * (at + 1))


def pair(at):
    return slice(2 * LANES * at, 2 * LANES * (at + 1))


def real_of(at):
    return slice(2 * LANES * at, 2 * LANES * at + LANES)


def imag_of(at):
    return slice(2 * LANES * at + LANES, 2 * LANES * (at + 1))


def put_left(left, at, real, imag):
    for columns, part in ((real_of(at), real), (imag_of(at), imag)):
        for ref, value in zip(left, split(part)):
            ref[:, columns] = value


def put_right(right, at, real, imag):
    for ref, r, i in zip(right, split(real), split(imag)):
        minus = -i
        for k in range(real.shape[0] // LANES):
            rows = cut(k)
            ref[real_of(k), real_of(at)] = r[rows]
            ref[real_of(k), imag_of(at)] = i[rows]
            ref[imag_of(k), real_of(at)] = minus[rows]
            ref[imag_of(k), imag_of(at)] = r[rows]


def product(left, right, epilogue, fill=()):
    for at in range(right[0].shape[1] // (2 * LANES)):
        columns = pair(at)
        high = right[0][:, columns]
        lh = left[0][...]
        value = jnp.dot(lh, high, preferred_element_type=F32)
        for low in right[1:]:
            value += jnp.dot(lh, low[:, columns], preferred_element_type=F32)
        for low in left[1:]:
            value += jnp.dot(low[...], high, preferred_element_type=F32)
        if at < len(fill):
            fill[at]()
        epilogue(at, value[:, :LANES], value[:, LANES:])


def storing(out):
    def epilogue(at, real, imag):
        out[:, real_of(at)] = real
        out[:, imag_of(at)] = imag

    return epilogue


def wide_chunk(ref, at):
    return ref[:, real_of(at)], ref[:, imag_of(at)]


def refined_inverse(chunk, left, first, second, rest, epilogue, fill=(), more=()):
    n = rest.shape[0]
    count = n // LANES
    on = lax.broadcasted_iota(jnp.int32, (LANES, LANES), 0) == lax.broadcasted_iota(
        jnp.int32, (LANES, LANES), 1
    )
    eye = on.astype(F32)
    column_parts = []
    for at in range(count):
        real, imag = chunk(at)
        tiles = [jnp.where(on, part[cut(at)], 0.0) for part in (real, imag)]
        pieces = []
        for axis in (0, 1):
            dr, di = [jnp.sum(t, axis=axis, keepdims=True) for t in tiles]
            modulus = dr * dr + di * di
            pieces.append((dr / modulus, -di / modulus))
        (xr, xi), column = pieces
        column_parts.append(column)
        m_real = real * xr - imag * xi
        m_imag = real * xi + imag * xr
        m_real = jnp.concatenate(
            [m_real[cut(k)] - eye if k == at else m_real[cut(k)] for k in range(count)], axis=0
        )
        put_left(left, at, m_real, m_imag)
        put_right(first, at, m_real, m_imag)
        rest[:, real_of(at)] = -m_real
        rest[:, imag_of(at)] = -m_imag

    def square(at, real, imag):
        put_right(second, at, real, imag)
        rest[:, real_of(at)] += real
        rest[:, imag_of(at)] += imag
        rest[cut(at), real_of(at)] += eye

    product(left, first, square, fill)
    col_real, col_imag = [
        jnp.concatenate([c[part] for c in column_parts], axis=0) for part in range(2)
    ]

    def finish(at, real, imag):
        q_real = rest[:, real_of(at)] - real
        q_imag = rest[:, imag_of(at)] - imag
        epilogue(at, col_real * q_real - col_imag * q_imag, col_real * q_imag + col_imag * q_real)

    product(left, second, finish, more)


def pairs_of(refs):
    return [(refs[i], refs[i + 1]) for i in range(0, len(refs), 2)]


def parity():
    return lax.axis_index("layer") % 2


def factors(which, coupling, left, right):
    is_even = which == 0

    def fill(at):
        def run():
            real, imag = coupling[0, :, cut(at)], coupling[1, :, cut(at)]
            real_t, imag_t = coupling[0, cut(at), :].T, -coupling[1, cut(at), :].T
            put_left(left, at, jnp.where(is_even, real, real_t), jnp.where(is_even, imag, imag_t))
            put_right(
                right, at, jnp.where(is_even, real_t, real), jnp.where(is_even, imag_t, imag)
            )

        return run

    return [fill(at) for at in range(coupling.shape[-1] // LANES)]


def sandwich(which, even, left, inverse, right, half, result, fill=()):
    is_even = which == 0
    product(left, inverse, lambda at, real, imag: put_left(half, at, real, imag), fill)

    def finish(at, real, imag):
        for part, (columns, term) in enumerate(((real_of(at), real), (imag_of(at), imag))):
            result[:, columns] = jnp.where(is_even, even[part, :, cut(at)] - term, term)

    product(half, right, finish)


def first_kernel(diag, couplings, *refs):
    inverse, right, half, far_left, far_right = pairs_of(refs[:10])
    even, border, odd, near, far, sems = refs[10:16]
    left, other, first, second = pairs_of(refs[16:24])
    rest = refs[24]
    which = parity()
    count = odd.shape[-1] // LANES
    urgent = [
        pltpu.make_async_copy(
            diag.at[0, 1, 0, part, cut(at)], odd.at[part, cut(at)], sems.at[part * count + at]
        )
        for part in range(2)
        for at in range(count)
    ]
    later = [
        pltpu.make_async_copy(couplings.at[0, which], near, sems.at[2 * count]),
        pltpu.make_async_copy(diag.at[0, 0, 0], even, sems.at[2 * count + 1]),
        pltpu.make_async_copy(couplings.at[0, 1 - which], far, sems.at[2 * count + 2]),
    ]
    for copy in urgent:
        copy.start()

    for copy in urgent:
        copy.wait()
    for copy in later:
        copy.start()

    def chunk(at):
        return odd[0, :, cut(at)], odd[1, :, cut(at)]

    def after(copy, runs):
        def start():
            copy.wait()
            runs[0]()

        return [start] + runs[1:]

    near_fill = factors(which, near, other, right)
    refined_inverse(
        chunk,
        left[:1],
        first[:1],
        second[:1],
        rest,
        lambda at, real, imag: put_right(inverse, at, real, imag),
        [lambda: None, after(later[0], near_fill[:1])[0], near_fill[1]],
        near_fill[2:],
    )
    later[1].wait()
    fill = after(later[2], factors(1 - which, far, far_left, far_right))
    sandwich(which, even, other, inverse, right, half, border, fill)


def second_kernel(even, *refs):
    inverse, left, right, half = pairs_of(refs[:8])
    sandwich(1 - parity(), even, left, inverse, right, half, refs[8])


def cross_kernel(*refs):
    slow, slow_right, fast, fast_right = pairs_of(refs[:8])
    one, two = refs[8:]
    product(slow, fast_right, lambda at, real, imag: storing(one)(at, -real, -imag))
    product(fast, slow_right, lambda at, real, imag: storing(two)(at, -real, -imag))


def reduced_term(chunk, before, after, rest, epilogue, scratch):
    left, other, first, second, third = scratch
    count = before.shape[0] // LANES
    refined_inverse(
        chunk,
        left[:1],
        first[:1],
        second[:1],
        rest,
        lambda at, real, imag: put_right(first, at, real, imag),
        [lambda at=at: put_left(other, at, *wide_chunk(before, at)) for at in range(count)],
        [lambda at=at: put_right(third, at, *wide_chunk(after, at)) for at in range(count)],
    )
    product(other, first, lambda at, real, imag: put_left(left, at, real, imag))
    product(left, third, epilogue)


def chip_kernel(mine, far, one, two, reduced, term, *refs):
    is_even = parity() == 0

    def chunk(at):
        parts = [
            jnp.where(is_even, b - a, a - b)
            for a, b in zip(wide_chunk(mine, at), wide_chunk(far, at))
        ]
        storing(reduced)(at, *parts)
        return parts

    reduced_term(chunk, one, two, refs[0], storing(term), pairs_of(refs[1:]))


def border_kernel(mine, far, one, two, reduced, chip_term, partial, term, *refs):
    index = lax.axis_index("layer")
    is_even = index % 2 == 0
    is_last = index == lax.axis_size("layer") - 1

    def chunk(at):
        parts = [
            jnp.where(is_even, a - b, b - a)
            for a, b in zip(wide_chunk(mine, at), wide_chunk(far, at))
        ]
        for columns, value in zip((real_of(at), imag_of(at)), parts):
            partial[:, columns] = jnp.where(
                is_even, value - chip_term[:, columns], reduced[:, columns]
            )
        return parts

    def finish(at, real, imag):
        for columns, value in ((real_of(at), real), (imag_of(at), imag)):
            value = jnp.where(is_last, 0.0, value)
            term[:, columns] = value
            partial[:, columns] -= jnp.where(is_even, 0.0, value)

    reduced_term(chunk, two, one, refs[0], finish, pairs_of(refs[1:]))


def greens_of(chunk, greens, refs):
    left, first, second = pairs_of(refs[1:])

    def finish(at, real, imag):
        greens[0, :, cut(at)] = real
        greens[1, :, cut(at)] = imag

    refined_inverse(chunk, left, first, second, refs[0], finish)


def weights_kernel(phonon, strength, transfer, offset, weights):
    energies, transfers = phonon.shape[0], transfer.shape[0]

    def put(row, value):
        weights[row : row + 1, :] = jnp.full((1, LANES), value, F32)

    for e in range(energies):
        for f in range(energies):
            put(e * energies + f, phonon[e, f])
    for q in range(transfers):
        mode = transfer[q]
        weight = strength[mode]
        still = offset[mode] == 0
        put(energies * energies + q, jnp.where(still, 2.0 * weight, 0.0))
        put(energies * energies + transfers + q, jnp.where(still, 0.0, weight))


def odd_greens_kernel(partial, chip_term, weights, greens, *refs):
    @pl.when(parity() == 1)
    def _():
        def chunk(at):
            return [a - b for a, b in zip(wide_chunk(partial, at), wide_chunk(chip_term, at))]

        greens_of(chunk, greens, refs)


def even_greens_kernel(partial, border_term, odd_greens, greens, *refs):
    @pl.when(parity() == 0)
    def _():
        def chunk(at):
            return [a - b for a, b in zip(wide_chunk(partial, at), wide_chunk(border_term, at))]

        greens_of(chunk, greens, refs)


def mix_kernel(weights, blocks, mixed):
    energies, momenta, depth, width = blocks.shape
    rows = [weights[row : row + 1, :] for row in range(energies * energies + 2 * momenta)]
    fold = [rows[e * energies : (e + 1) * energies] for e in range(energies)]
    stay, move = rows[-2 * momenta : -momenta], rows[-momenta:]
    for at in range(0, width, 128):
        columns = slice(at, at + 128)

        def rows_of(i, carry):
            rows = pl.ds(pl.multiple_of(i * 8, 8), 8)
            folded = []
            for k in range(momenta):
                g = [blocks[f, k, rows, columns] for f in range(energies)]
                folded.append(
                    [sum(fold[e][f] * g[f] for f in range(energies)) for e in range(energies)]
                )
            for k in range(momenta):
                moved = [
                    sum(move[q] * folded[(k - q) % momenta][e] for q in range(momenta))
                    for e in range(energies)
                ]
                for e in range(energies):
                    total = sum(stay[q] * folded[(k - q) % momenta][e] for q in range(momenta))
                    if e > 0:
                        total = total + moved[e - 1]
                    if e + 1 < energies:
                        total = total + moved[e + 1]
                    mixed[e, k, rows, columns] = total
            return carry

        lax.fori_loop(0, depth // 8, rows_of, 0, unroll=2)


def call(kernel, outs, operands, scratch=(), aliases=()):
    def spec(value):
        if value.ndim > 3:
            return pl.BlockSpec(memory_space=pl.ANY)
        if value.shape[-1] < LANES:
            return pl.BlockSpec(memory_space=pltpu.SMEM)
        return pl.BlockSpec(memory_space=pltpu.VMEM)

    return pl.pallas_call(
        kernel,
        out_shape=outs,
        in_specs=[spec(o) for o in operands],
        out_specs=[spec(o) for o in outs],
        scratch_shapes=list(scratch),
        input_output_aliases=dict(aliases),
        compiler_params=pltpu.CompilerParams(vmem_limit_bytes=20 * 1024 * 1024),
        cost_estimate=pl.CostEstimate(flops=COST[kernel.__name__], bytes_accessed=1, transcendentals=0),
    )(*operands)


def swap(block, axis, first):
    route = []
    for i in range(first, lax.axis_size(axis) - 1, 2):
        route += [(i, i + 1), (i + 1, i)]
    return lax.ppermute(block, axis, route)


def ahead(block, axis, first):
    return lax.ppermute(
        block, axis, [(i, i + 1) for i in range(first, lax.axis_size(axis) - 1, 2)]
    )


def body(diag_blocks, couplings, phonon_matrix, mode_strength, transfer_mode, energy_offset):
    n = diag_blocks.shape[-1]
    wide = jax.ShapeDtypeStruct((n, 2 * n), F32)
    square = jax.ShapeDtypeStruct((2, n, n), F32)
    left = [jax.ShapeDtypeStruct((n, 2 * n), BF16)] * 2
    right = [jax.ShapeDtypeStruct((2 * n, 2 * n), BF16)] * 2
    flat = [pltpu.VMEM((n, 2 * n), F32)]
    block = [pltpu.VMEM((2, n, n), F32)]
    lefts = [pltpu.VMEM((n, 2 * n), BF16)] * 2
    rights = [pltpu.VMEM((2 * n, 2 * n), BF16)] * 2

    diag_blocks, couplings = [
        pltpu.with_memory_space_constraint(v, pltpu.HBM) for v in (diag_blocks, couplings)
    ]
    *parts, even, border = call(
        first_kernel,
        right + right + left + left + right + [square, wide],
        (diag_blocks, couplings),
        block * 3 + [pltpu.SemaphoreType.DMA((2 * (n // LANES) + 3,))] + lefts * 2 + rights * 2 + flat,
    )
    inverse, slow_right, slow, fast_left, fast_right = [parts[i : i + 2] for i in range(0, 10, 2)]
    border_far = swap(border, "layer", 1)
    *fast, chip = call(
        second_kernel, left + [wide], (even, *inverse, *fast_left, *fast_right)
    )
    chip, border = lax.optimization_barrier((chip, border))
    chip_far = swap(chip, "layer", 0)
    one, two = call(cross_kernel, [wide] * 2, (*slow, *slow_right, *fast, *fast_right))
    scratch = flat + lefts * 2 + rights * 3
    reduced, chip_term = call(chip_kernel, [wide] * 2, (chip, chip_far, one, two), scratch)
    from_border = ahead(chip_term, "layer", 1)
    partial, border_term = call(
        border_kernel, [wide] * 2, (border, border_far, one, two, reduced, chip_term), scratch
    )
    from_chip = ahead(border_term, "layer", 0)
    energies, momenta = lax.axis_size("energy"), lax.axis_size("momentum")
    table = jax.ShapeDtypeStruct((energies * energies + 2 * momenta, LANES), F32)
    (weights,) = call(
        weights_kernel, [table], (phonon_matrix, mode_strength, transfer_mode, energy_offset)
    )
    scratch = flat + lefts + rights * 2
    (greens,) = call(odd_greens_kernel, [square], (partial, from_chip, weights), scratch)
    (greens,) = call(
        even_greens_kernel, [square], (partial, from_border, greens), scratch, aliases={2: 0}
    )
    group = energies * momenta
    depth = 2 * n // group
    axes = ("energy", "momentum")
    spread = lax.all_to_all(
        greens.reshape(group, depth, n), axes, split_axis=0, concat_axis=0, tiled=True
    )
    block = (energies, momenta, depth, n)
    mixed = pl.pallas_call(
        mix_kernel,
        out_shape=jax.ShapeDtypeStruct(block, F32),
        in_specs=[pl.BlockSpec(memory_space=pltpu.VMEM)] * 2,
        out_specs=pl.BlockSpec(memory_space=pltpu.VMEM),
        compiler_params=pltpu.CompilerParams(vmem_limit_bytes=12 * 1024 * 1024),
    )(weights, spread.reshape(block))
    returned = lax.all_to_all(
        mixed.reshape(group, depth, n), axes, split_axis=0, concat_axis=0, tiled=True
    )
    return returned.reshape(1, 1, 1, 2, n, n)


COST = dict(weights_kernel=3 * 10**10, first_kernel=3 * 10**10, second_kernel=3 * 10**10, cross_kernel=3 * 10**10, chip_kernel=3 * 10**10, border_kernel=3 * 10**10, odd_greens_kernel=1, even_greens_kernel=3 * 10**10)


def solution(mesh):
    return jax.shard_map(
        body,
        mesh=mesh,
        in_specs=(
            P("momentum", "layer", "energy", None, None, None),
            P("momentum", "layer", None, None, None),
            P(),
            P(),
            P(),
            P(),
        ),
        out_specs=P("momentum", "layer", "energy", None, None, None),
        check_vma=False,
    )
```

```python
import jax
import jax.numpy as jnp
from jax import lax
from jax.experimental import pallas as pl
from jax.experimental.pallas import tpu as pltpu
from jax.sharding import PartitionSpec as P

F32 = jnp.float32
BF16 = jnp.bfloat16


def split(value):
    high = value.astype(BF16)
    return high, (value - high.astype(F32)).astype(BF16)


LANES = 128


def cut(at):
    return slice(LANES * at, LANES * (at + 1))


def pair(at):
    return slice(2 * LANES * at, 2 * LANES * (at + 1))


def real_of(at):
    return slice(2 * LANES * at, 2 * LANES * at + LANES)


def imag_of(at):
    return slice(2 * LANES * at + LANES, 2 * LANES * (at + 1))


def put_left(left, at, real, imag):
    for columns, part in ((real_of(at), real), (imag_of(at), imag)):
        for ref, value in zip(left, split(part)):
            ref[:, columns] = value


def put_right(right, at, real, imag):
    for ref, r, i in zip(right, split(real), split(imag)):
        minus = -i
        for k in range(real.shape[0] // LANES):
            rows = cut(k)
            ref[real_of(k), real_of(at)] = r[rows]
            ref[real_of(k), imag_of(at)] = i[rows]
            ref[imag_of(k), real_of(at)] = minus[rows]
            ref[imag_of(k), imag_of(at)] = r[rows]


def product(left, right, epilogue, fill=()):
    for at in range(right[0].shape[1] // (2 * LANES)):
        columns = pair(at)
        high = right[0][:, columns]
        lh = left[0][...]
        value = jnp.dot(lh, high, preferred_element_type=F32)
        for low in right[1:]:
            value += jnp.dot(lh, low[:, columns], preferred_element_type=F32)
        for low in left[1:]:
            value += jnp.dot(low[...], high, preferred_element_type=F32)
        if at < len(fill):
            fill[at]()
        epilogue(at, value[:, :LANES], value[:, LANES:])


def storing(out):
    def epilogue(at, real, imag):
        out[:, real_of(at)] = real
        out[:, imag_of(at)] = imag

    return epilogue


def wide_chunk(ref, at):
    return ref[:, real_of(at)], ref[:, imag_of(at)]


def refined_inverse(chunk, left, first, second, rest, epilogue, fill=(), more=()):
    n = rest.shape[0]
    count = n // LANES
    on = lax.broadcasted_iota(jnp.int32, (LANES, LANES), 0) == lax.broadcasted_iota(
        jnp.int32, (LANES, LANES), 1
    )
    eye = on.astype(F32)
    column_parts = []
    for at in range(count):
        real, imag = chunk(at)
        tiles = [jnp.where(on, part[cut(at)], 0.0) for part in (real, imag)]
        pieces = []
        for axis in (0, 1):
            dr, di = [jnp.sum(t, axis=axis, keepdims=True) for t in tiles]
            modulus = dr * dr + di * di
            pieces.append((dr / modulus, -di / modulus))
        (xr, xi), column = pieces
        column_parts.append(column)
        m_real = real * xr - imag * xi
        m_imag = real * xi + imag * xr
        m_real = jnp.concatenate(
            [m_real[cut(k)] - eye if k == at else m_real[cut(k)] for k in range(count)], axis=0
        )
        put_left(left, at, m_real, m_imag)
        put_right(first, at, m_real, m_imag)
        rest[:, real_of(at)] = -m_real
        rest[:, imag_of(at)] = -m_imag

    def square(at, real, imag):
        put_right(second, at, real, imag)
        rest[:, real_of(at)] += real
        rest[:, imag_of(at)] += imag
        rest[cut(at), real_of(at)] += eye

    product(left, first, square, fill)
    col_real, col_imag = [
        jnp.concatenate([c[part] for c in column_parts], axis=0) for part in range(2)
    ]

    def finish(at, real, imag):
        q_real = rest[:, real_of(at)] - real
        q_imag = rest[:, imag_of(at)] - imag
        epilogue(at, col_real * q_real - col_imag * q_imag, col_real * q_imag + col_imag * q_real)

    product(left, second, finish, more)


def pairs_of(refs):
    return [(refs[i], refs[i + 1]) for i in range(0, len(refs), 2)]


def parity():
    return lax.axis_index("layer") % 2


def factors(which, coupling, left, right):
    is_even = which == 0

    def fill(at):
        def run():
            real, imag = coupling[0, :, cut(at)], coupling[1, :, cut(at)]
            real_t, imag_t = coupling[0, cut(at), :].T, -coupling[1, cut(at), :].T
            put_left(left, at, jnp.where(is_even, real, real_t), jnp.where(is_even, imag, imag_t))
            put_right(
                right, at, jnp.where(is_even, real_t, real), jnp.where(is_even, imag_t, imag)
            )

        return run

    return [fill(at) for at in range(coupling.shape[-1] // LANES)]


def sandwich(which, even, left, inverse, right, half, result, fill=()):
    is_even = which == 0
    product(left, inverse, lambda at, real, imag: put_left(half, at, real, imag), fill)

    def finish(at, real, imag):
        for part, (columns, term) in enumerate(((real_of(at), real), (imag_of(at), imag))):
            result[:, columns] = jnp.where(is_even, even[part, :, cut(at)] - term, term)

    product(half, right, finish)


def first_kernel(diag, couplings, *refs):
    inverse, right, half, far_left, far_right = pairs_of(refs[:10])
    even, border, odd, near, far, sems = refs[10:16]
    left, other, first, second = pairs_of(refs[16:24])
    rest = refs[24]
    which = parity()
    count = odd.shape[-1] // LANES
    urgent = [
        pltpu.make_async_copy(
            diag.at[0, 1, 0, part, cut(at)], odd.at[part, cut(at)], sems.at[part * count + at]
        )
        for part in range(2)
        for at in range(count)
    ]
    later = [
        pltpu.make_async_copy(couplings.at[0, which], near, sems.at[2 * count]),
        pltpu.make_async_copy(diag.at[0, 0, 0], even, sems.at[2 * count + 1]),
        pltpu.make_async_copy(couplings.at[0, 1 - which], far, sems.at[2 * count + 2]),
    ]
    for copy in urgent:
        copy.start()

    later[0].start()
    for copy in urgent:
        copy.wait()
    for copy in later[1:]:
        copy.start()

    def chunk(at):
        return odd[0, :, cut(at)], odd[1, :, cut(at)]

    def after(copy, runs):
        def start():
            copy.wait()
            runs[0]()

        return [start] + runs[1:]

    near_fill = factors(which, near, other, right)
    refined_inverse(
        chunk,
        left[:1],
        first[:1],
        second[:1],
        rest,
        lambda at, real, imag: put_right(inverse, at, real, imag),
        [lambda: None, after(later[0], near_fill[:1])[0], near_fill[1]],
        near_fill[2:],
    )
    later[1].wait()
    fill = after(later[2], factors(1 - which, far, far_left, far_right))
    sandwich(which, even, other, inverse, right, half, border, fill)


def second_kernel(even, *refs):
    inverse, left, right, half = pairs_of(refs[:8])
    sandwich(1 - parity(), even, left, inverse, right, half, refs[8])


def cross_kernel(*refs):
    slow, slow_right, fast, fast_right = pairs_of(refs[:8])
    one, two = refs[8:]
    product(slow, fast_right, lambda at, real, imag: storing(one)(at, -real, -imag))
    product(fast, slow_right, lambda at, real, imag: storing(two)(at, -real, -imag))


def reduced_term(chunk, before, after, rest, epilogue, scratch):
    left, other, first, second, third = scratch
    count = before.shape[0] // LANES
    refined_inverse(
        chunk,
        left[:1],
        first[:1],
        second[:1],
        rest,
        lambda at, real, imag: put_right(first, at, real, imag),
        [lambda at=at: put_left(other, at, *wide_chunk(before, at)) for at in range(count)],
        [lambda at=at: put_right(third, at, *wide_chunk(after, at)) for at in range(count)],
    )
    product(other, first, lambda at, real, imag: put_left(left, at, real, imag))
    product(left, third, epilogue)


def chip_kernel(mine, far, one, two, reduced, term, *refs):
    is_even = parity() == 0

    def chunk(at):
        parts = [
            jnp.where(is_even, b - a, a - b)
            for a, b in zip(wide_chunk(mine, at), wide_chunk(far, at))
        ]
        storing(reduced)(at, *parts)
        return parts

    reduced_term(chunk, one, two, refs[0], storing(term), pairs_of(refs[1:]))


def border_kernel(mine, far, one, two, reduced, chip_term, partial, term, *refs):
    index = lax.axis_index("layer")
    is_even = index % 2 == 0
    is_last = index == lax.axis_size("layer") - 1

    def chunk(at):
        parts = [
            jnp.where(is_even, a - b, b - a)
            for a, b in zip(wide_chunk(mine, at), wide_chunk(far, at))
        ]
        for columns, value in zip((real_of(at), imag_of(at)), parts):
            partial[:, columns] = jnp.where(
                is_even, value - chip_term[:, columns], reduced[:, columns]
            )
        return parts

    def finish(at, real, imag):
        for columns, value in ((real_of(at), real), (imag_of(at), imag)):
            value = jnp.where(is_last, 0.0, value)
            term[:, columns] = value
            partial[:, columns] -= jnp.where(is_even, 0.0, value)

    reduced_term(chunk, two, one, refs[0], finish, pairs_of(refs[1:]))


def greens_of(chunk, greens, refs):
    left, first, second = pairs_of(refs[1:])

    def finish(at, real, imag):
        greens[0, :, cut(at)] = real
        greens[1, :, cut(at)] = imag

    refined_inverse(chunk, left, first, second, refs[0], finish)


def weights_kernel(phonon, strength, transfer, offset, weights):
    energies, transfers = phonon.shape[0], transfer.shape[0]

    def put(row, value):
        weights[row : row + 1, :] = jnp.full((1, LANES), value, F32)

    for e in range(energies):
        for f in range(energies):
            put(e * energies + f, phonon[e, f])
    for q in range(transfers):
        mode = transfer[q]
        weight = strength[mode]
        still = offset[mode] == 0
        put(energies * energies + q, jnp.where(still, 2.0 * weight, 0.0))
        put(energies * energies + transfers + q, jnp.where(still, 0.0, weight))


def odd_greens_kernel(partial, chip_term, weights, greens, *refs):
    @pl.when(parity() == 1)
    def _():
        def chunk(at):
            return [a - b for a, b in zip(wide_chunk(partial, at), wide_chunk(chip_term, at))]

        greens_of(chunk, greens, refs)


def even_greens_kernel(partial, border_term, odd_greens, greens, *refs):
    @pl.when(parity() == 0)
    def _():
        def chunk(at):
            return [a - b for a, b in zip(wide_chunk(partial, at), wide_chunk(border_term, at))]

        greens_of(chunk, greens, refs)


def mix_kernel(weights, blocks, mixed):
    energies, momenta, depth, width = blocks.shape
    rows = [weights[row : row + 1, :] for row in range(energies * energies + 2 * momenta)]
    fold = [rows[e * energies : (e + 1) * energies] for e in range(energies)]
    stay, move = rows[-2 * momenta : -momenta], rows[-momenta:]
    for at in range(0, width, 128):
        columns = slice(at, at + 128)

        def rows_of(i, carry):
            rows = pl.ds(pl.multiple_of(i * 8, 8), 8)
            folded = []
            for k in range(momenta):
                g = [blocks[f, k, rows, columns] for f in range(energies)]
                folded.append(
                    [sum(fold[e][f] * g[f] for f in range(energies)) for e in range(energies)]
                )
            for k in range(momenta):
                moved = [
                    sum(move[q] * folded[(k - q) % momenta][e] for q in range(momenta))
                    for e in range(energies)
                ]
                for e in range(energies):
                    total = sum(stay[q] * folded[(k - q) % momenta][e] for q in range(momenta))
                    if e > 0:
                        total = total + moved[e - 1]
                    if e + 1 < energies:
                        total = total + moved[e + 1]
                    mixed[e, k, rows, columns] = total
            return carry

        lax.fori_loop(0, depth // 8, rows_of, 0, unroll=True)


def call(kernel, outs, operands, scratch=(), aliases=()):
    def spec(value):
        if value.ndim > 3:
            return pl.BlockSpec(memory_space=pl.ANY)
        if value.shape[-1] < LANES:
            return pl.BlockSpec(memory_space=pltpu.SMEM)
        return pl.BlockSpec(memory_space=pltpu.VMEM)

    return pl.pallas_call(
        kernel,
        out_shape=outs,
        in_specs=[spec(o) for o in operands],
        out_specs=[spec(o) for o in outs],
        scratch_shapes=list(scratch),
        input_output_aliases=dict(aliases),
        compiler_params=pltpu.CompilerParams(vmem_limit_bytes=20 * 1024 * 1024),
        cost_estimate=pl.CostEstimate(flops=COST[kernel.__name__], bytes_accessed=1, transcendentals=0),
    )(*operands)


def swap(block, axis, first):
    route = []
    for i in range(first, lax.axis_size(axis) - 1, 2):
        route += [(i, i + 1), (i + 1, i)]
    return lax.ppermute(block, axis, route)


def ahead(block, axis, first):
    return lax.ppermute(
        block, axis, [(i, i + 1) for i in range(first, lax.axis_size(axis) - 1, 2)]
    )


def body(diag_blocks, couplings, phonon_matrix, mode_strength, transfer_mode, energy_offset):
    n = diag_blocks.shape[-1]
    wide = jax.ShapeDtypeStruct((n, 2 * n), F32)
    square = jax.ShapeDtypeStruct((2, n, n), F32)
    left = [jax.ShapeDtypeStruct((n, 2 * n), BF16)] * 2
    right = [jax.ShapeDtypeStruct((2 * n, 2 * n), BF16)] * 2
    flat = [pltpu.VMEM((n, 2 * n), F32)]
    block = [pltpu.VMEM((2, n, n), F32)]
    lefts = [pltpu.VMEM((n, 2 * n), BF16)] * 2
    rights = [pltpu.VMEM((2 * n, 2 * n), BF16)] * 2

    diag_blocks, couplings = [
        pltpu.with_memory_space_constraint(v, pltpu.HBM) for v in (diag_blocks, couplings)
    ]
    *parts, even, border = call(
        first_kernel,
        right + right + left + left + right + [square, wide],
        (diag_blocks, couplings),
        block * 3 + [pltpu.SemaphoreType.DMA((2 * (n // LANES) + 3,))] + lefts * 2 + rights * 2 + flat,
    )
    inverse, slow_right, slow, fast_left, fast_right = [parts[i : i + 2] for i in range(0, 10, 2)]
    border_far = swap(border, "layer", 1)
    *fast, chip = call(
        second_kernel, left + [wide], (even, *inverse, *fast_left, *fast_right)
    )
    chip, border = lax.optimization_barrier((chip, border))
    chip_far = swap(chip, "layer", 0)
    one, two = call(cross_kernel, [wide] * 2, (*slow, *slow_right, *fast, *fast_right))
    scratch = flat + lefts * 2 + rights * 3
    reduced, chip_term = call(chip_kernel, [wide] * 2, (chip, chip_far, one, two), scratch)
    from_border = ahead(chip_term, "layer", 1)
    partial, border_term = call(
        border_kernel, [wide] * 2, (border, border_far, one, two, reduced, chip_term), scratch
    )
    from_chip = ahead(border_term, "layer", 0)
    energies, momenta = lax.axis_size("energy"), lax.axis_size("momentum")
    table = jax.ShapeDtypeStruct((energies * energies + 2 * momenta, LANES), F32)
    (weights,) = call(
        weights_kernel, [table], (phonon_matrix, mode_strength, transfer_mode, energy_offset)
    )
    scratch = flat + lefts + rights * 2
    (greens,) = call(odd_greens_kernel, [square], (partial, from_chip, weights), scratch)
    (greens,) = call(
        even_greens_kernel, [square], (partial, from_border, greens), scratch, aliases={2: 0}
    )
    group = energies * momenta
    depth = 2 * n // group
    axes = ("energy", "momentum")
    spread = lax.all_to_all(
        greens.reshape(group, depth, n), axes, split_axis=0, concat_axis=0, tiled=True
    )
    block = (energies, momenta, depth, n)
    mixed = pl.pallas_call(
        mix_kernel,
        out_shape=jax.ShapeDtypeStruct(block, F32),
        in_specs=[pl.BlockSpec(memory_space=pltpu.VMEM)] * 2,
        out_specs=pl.BlockSpec(memory_space=pltpu.VMEM),
        compiler_params=pltpu.CompilerParams(vmem_limit_bytes=12 * 1024 * 1024),
    )(weights, spread.reshape(block))
    returned = lax.all_to_all(
        mixed.reshape(group, depth, n), axes, split_axis=0, concat_axis=0, tiled=True
    )
    return returned.reshape(1, 1, 1, 2, n, n)


COST = dict(weights_kernel=3 * 10**10, first_kernel=3 * 10**10, second_kernel=3 * 10**10, cross_kernel=3 * 10**10, chip_kernel=3 * 10**10, border_kernel=3 * 10**10, odd_greens_kernel=1, even_greens_kernel=3 * 10**10)


def solution(mesh):
    return jax.shard_map(
        body,
        mesh=mesh,
        in_specs=(
            P("momentum", "layer", "energy", None, None, None),
            P("momentum", "layer", None, None, None),
            P(),
            P(),
            P(),
            P(),
        ),
        out_specs=P("momentum", "layer", "energy", None, None, None),
        check_vma=False,
    )
```

```python
import jax
import jax.numpy as jnp
from jax import lax
from jax.experimental import pallas as pl
from jax.experimental.pallas import tpu as pltpu
from jax.sharding import PartitionSpec as P

F32 = jnp.float32
BF16 = jnp.bfloat16


def split(value):
    high = value.astype(BF16)
    return high, (value - high.astype(F32)).astype(BF16)


LANES = 128


def cut(at):
    return slice(LANES * at, LANES * (at + 1))


def pair(at):
    return slice(2 * LANES * at, 2 * LANES * (at + 1))


def real_of(at):
    return slice(2 * LANES * at, 2 * LANES * at + LANES)


def imag_of(at):
    return slice(2 * LANES * at + LANES, 2 * LANES * (at + 1))


def put_left(left, at, real, imag):
    for columns, part in ((real_of(at), real), (imag_of(at), imag)):
        for ref, value in zip(left, split(part)):
            ref[:, columns] = value


def put_right(right, at, real, imag):
    for ref, r, i in zip(right, split(real), split(imag)):
        minus = -i
        for k in range(real.shape[0] // LANES):
            rows = cut(k)
            ref[real_of(k), real_of(at)] = r[rows]
            ref[real_of(k), imag_of(at)] = i[rows]
            ref[imag_of(k), real_of(at)] = minus[rows]
            ref[imag_of(k), imag_of(at)] = r[rows]


def product(left, right, epilogue, fill=()):
    for at in range(right[0].shape[1] // (2 * LANES)):
        columns = pair(at)
        high = right[0][:, columns]
        lh = left[0][...]
        value = jnp.dot(lh, high, preferred_element_type=F32)
        for low in right[1:]:
            value += jnp.dot(lh, low[:, columns], preferred_element_type=F32)
        for low in left[1:]:
            value += jnp.dot(low[...], high, preferred_element_type=F32)
        if at < len(fill):
            fill[at]()
        epilogue(at, value[:, :LANES], value[:, LANES:])


def storing(out):
    def epilogue(at, real, imag):
        out[:, real_of(at)] = real
        out[:, imag_of(at)] = imag

    return epilogue


def wide_chunk(ref, at):
    return ref[:, real_of(at)], ref[:, imag_of(at)]


def refined_inverse(chunk, left, first, second, rest, epilogue, fill=(), more=()):
    n = rest.shape[0]
    count = n // LANES
    on = lax.broadcasted_iota(jnp.int32, (LANES, LANES), 0) == lax.broadcasted_iota(
        jnp.int32, (LANES, LANES), 1
    )
    eye = on.astype(F32)
    column_parts = []
    for at in range(count):
        real, imag = chunk(at)
        tiles = [jnp.where(on, part[cut(at)], 0.0) for part in (real, imag)]
        pieces = []
        for axis in (0, 1):
            dr, di = [jnp.sum(t, axis=axis, keepdims=True) for t in tiles]
            modulus = dr * dr + di * di
            pieces.append((dr / modulus, -di / modulus))
        (xr, xi), column = pieces
        column_parts.append(column)
        m_real = real * xr - imag * xi
        m_imag = real * xi + imag * xr
        m_real = jnp.concatenate(
            [m_real[cut(k)] - eye if k == at else m_real[cut(k)] for k in range(count)], axis=0
        )
        put_left(left, at, m_real, m_imag)
        put_right(first, at, m_real, m_imag)
        rest[:, real_of(at)] = -m_real
        rest[:, imag_of(at)] = -m_imag

    def square(at, real, imag):
        put_right(second, at, real, imag)
        rest[:, real_of(at)] += real
        rest[:, imag_of(at)] += imag
        rest[cut(at), real_of(at)] += eye

    product(left, first, square, fill)
    col_real, col_imag = [
        jnp.concatenate([c[part] for c in column_parts], axis=0) for part in range(2)
    ]

    def finish(at, real, imag):
        q_real = rest[:, real_of(at)] - real
        q_imag = rest[:, imag_of(at)] - imag
        epilogue(at, col_real * q_real - col_imag * q_imag, col_real * q_imag + col_imag * q_real)

    product(left[: len(second)], second, finish, more)


def pairs_of(refs):
    return [(refs[i], refs[i + 1]) for i in range(0, len(refs), 2)]


def parity():
    return lax.axis_index("layer") % 2


def factors(which, coupling, left, right):
    is_even = which == 0

    def fill(at):
        def run():
            real, imag = coupling[0, :, cut(at)], coupling[1, :, cut(at)]
            real_t, imag_t = coupling[0, cut(at), :].T, -coupling[1, cut(at), :].T
            put_left(left, at, jnp.where(is_even, real, real_t), jnp.where(is_even, imag, imag_t))
            put_right(
                right, at, jnp.where(is_even, real_t, real), jnp.where(is_even, imag_t, imag)
            )

        return run

    return [fill(at) for at in range(coupling.shape[-1] // LANES)]


def sandwich(which, even, left, inverse, right, half, result, fill=()):
    is_even = which == 0
    product(left, inverse, lambda at, real, imag: put_left(half, at, real, imag), fill)

    def finish(at, real, imag):
        for part, (columns, term) in enumerate(((real_of(at), real), (imag_of(at), imag))):
            result[:, columns] = jnp.where(is_even, even[part, :, cut(at)] - term, term)

    product(half, right, finish)


def first_kernel(diag, couplings, *refs):
    inverse, right, half, far_left, far_right = pairs_of(refs[:10])
    even, border, odd, near, far, sems = refs[10:16]
    left, other, first, second = pairs_of(refs[16:24])
    rest = refs[24]
    which = parity()
    count = odd.shape[-1] // LANES
    urgent = [
        pltpu.make_async_copy(
            diag.at[0, 1, 0, part, cut(at)], odd.at[part, cut(at)], sems.at[part * count + at]
        )
        for part in range(2)
        for at in range(count)
    ]
    later = [
        pltpu.make_async_copy(couplings.at[0, which], near, sems.at[2 * count]),
        pltpu.make_async_copy(diag.at[0, 0, 0], even, sems.at[2 * count + 1]),
        pltpu.make_async_copy(couplings.at[0, 1 - which], far, sems.at[2 * count + 2]),
    ]
    for copy in urgent:
        copy.start()

    later[0].start()
    for copy in urgent:
        copy.wait()
    for copy in later[1:]:
        copy.start()

    def chunk(at):
        return odd[0, :, cut(at)], odd[1, :, cut(at)]

    def after(copy, runs):
        def start():
            copy.wait()
            runs[0]()

        return [start] + runs[1:]

    near_fill = factors(which, near, other, right)
    refined_inverse(
        chunk,
        left,
        first,
        second[:1],
        rest,
        lambda at, real, imag: put_right(inverse, at, real, imag),
        [lambda: None, after(later[0], near_fill[:1])[0], near_fill[1]],
        near_fill[2:],
    )
    later[1].wait()
    fill = after(later[2], factors(1 - which, far, far_left, far_right))
    sandwich(which, even, other, inverse, right, half, border, fill)


def second_kernel(even, *refs):
    inverse, left, right, half = pairs_of(refs[:8])
    sandwich(1 - parity(), even, left, inverse, right, half, refs[8])


def cross_kernel(*refs):
    slow, slow_right, fast, fast_right = pairs_of(refs[:8])
    one, two = refs[8:]
    product(slow, fast_right, lambda at, real, imag: storing(one)(at, -real, -imag))
    product(fast, slow_right, lambda at, real, imag: storing(two)(at, -real, -imag))


def reduced_term(chunk, before, after, rest, epilogue, scratch):
    left, other, first, second, third = scratch
    count = before.shape[0] // LANES
    refined_inverse(
        chunk,
        left[:1],
        first[:1],
        second[:1],
        rest,
        lambda at, real, imag: put_right(first, at, real, imag),
        [lambda at=at: put_left(other, at, *wide_chunk(before, at)) for at in range(count)],
        [lambda at=at: put_right(third, at, *wide_chunk(after, at)) for at in range(count)],
    )
    product(other, first, lambda at, real, imag: put_left(left, at, real, imag))
    product(left, third, epilogue)


def chip_kernel(mine, far, one, two, reduced, term, *refs):
    is_even = parity() == 0

    def chunk(at):
        parts = [
            jnp.where(is_even, b - a, a - b)
            for a, b in zip(wide_chunk(mine, at), wide_chunk(far, at))
        ]
        storing(reduced)(at, *parts)
        return parts

    reduced_term(chunk, one, two, refs[0], storing(term), pairs_of(refs[1:]))


def border_kernel(mine, far, one, two, reduced, chip_term, partial, term, *refs):
    index = lax.axis_index("layer")
    is_even = index % 2 == 0
    is_last = index == lax.axis_size("layer") - 1

    def chunk(at):
        parts = [
            jnp.where(is_even, a - b, b - a)
            for a, b in zip(wide_chunk(mine, at), wide_chunk(far, at))
        ]
        for columns, value in zip((real_of(at), imag_of(at)), parts):
            partial[:, columns] = jnp.where(
                is_even, value - chip_term[:, columns], reduced[:, columns]
            )
        return parts

    def finish(at, real, imag):
        for columns, value in ((real_of(at), real), (imag_of(at), imag)):
            value = jnp.where(is_last, 0.0, value)
            term[:, columns] = value
            partial[:, columns] -= jnp.where(is_even, 0.0, value)

    reduced_term(chunk, two, one, refs[0], finish, pairs_of(refs[1:]))


def greens_of(chunk, greens, refs):
    left, first, second = pairs_of(refs[1:])

    def finish(at, real, imag):
        greens[0, :, cut(at)] = real
        greens[1, :, cut(at)] = imag

    refined_inverse(chunk, left, first, second, refs[0], finish)


def weights_kernel(phonon, strength, transfer, offset, weights):
    energies, transfers = phonon.shape[0], transfer.shape[0]

    def put(row, value):
        weights[row : row + 1, :] = jnp.full((1, LANES), value, F32)

    for e in range(energies):
        for f in range(energies):
            put(e * energies + f, phonon[e, f])
    for q in range(transfers):
        mode = transfer[q]
        weight = strength[mode]
        still = offset[mode] == 0
        put(energies * energies + q, jnp.where(still, 2.0 * weight, 0.0))
        put(energies * energies + transfers + q, jnp.where(still, 0.0, weight))


def odd_greens_kernel(partial, chip_term, weights, greens, *refs):
    @pl.when(parity() == 1)
    def _():
        def chunk(at):
            return [a - b for a, b in zip(wide_chunk(partial, at), wide_chunk(chip_term, at))]

        greens_of(chunk, greens, refs)


def even_greens_kernel(partial, border_term, odd_greens, greens, *refs):
    @pl.when(parity() == 0)
    def _():
        def chunk(at):
            return [a - b for a, b in zip(wide_chunk(partial, at), wide_chunk(border_term, at))]

        greens_of(chunk, greens, refs)


def mix_kernel(weights, blocks, mixed):
    energies, momenta, depth, width = blocks.shape
    rows = [weights[row : row + 1, :] for row in range(energies * energies + 2 * momenta)]
    fold = [rows[e * energies : (e + 1) * energies] for e in range(energies)]
    stay, move = rows[-2 * momenta : -momenta], rows[-momenta:]
    for at in range(0, width, 128):
        columns = slice(at, at + 128)

        def rows_of(i, carry):
            rows = pl.ds(pl.multiple_of(i * 8, 8), 8)
            folded = []
            for k in range(momenta):
                g = [blocks[f, k, rows, columns] for f in range(energies)]
                folded.append(
                    [sum(fold[e][f] * g[f] for f in range(energies)) for e in range(energies)]
                )
            for k in range(momenta):
                moved = [
                    sum(move[q] * folded[(k - q) % momenta][e] for q in range(momenta))
                    for e in range(energies)
                ]
                for e in range(energies):
                    total = sum(stay[q] * folded[(k - q) % momenta][e] for q in range(momenta))
                    if e > 0:
                        total = total + moved[e - 1]
                    if e + 1 < energies:
                        total = total + moved[e + 1]
                    mixed[e, k, rows, columns] = total
            return carry

        lax.fori_loop(0, depth // 8, rows_of, 0, unroll=True)


def call(kernel, outs, operands, scratch=(), aliases=()):
    def spec(value):
        if value.ndim > 3:
            return pl.BlockSpec(memory_space=pl.ANY)
        if value.shape[-1] < LANES:
            return pl.BlockSpec(memory_space=pltpu.SMEM)
        return pl.BlockSpec(memory_space=pltpu.VMEM)

    return pl.pallas_call(
        kernel,
        out_shape=outs,
        in_specs=[spec(o) for o in operands],
        out_specs=[spec(o) for o in outs],
        scratch_shapes=list(scratch),
        input_output_aliases=dict(aliases),
        compiler_params=pltpu.CompilerParams(vmem_limit_bytes=20 * 1024 * 1024),
        cost_estimate=pl.CostEstimate(flops=COST[kernel.__name__], bytes_accessed=1, transcendentals=0),
    )(*operands)


def swap(block, axis, first):
    route = []
    for i in range(first, lax.axis_size(axis) - 1, 2):
        route += [(i, i + 1), (i + 1, i)]
    return lax.ppermute(block, axis, route)


def ahead(block, axis, first):
    return lax.ppermute(
        block, axis, [(i, i + 1) for i in range(first, lax.axis_size(axis) - 1, 2)]
    )


def body(diag_blocks, couplings, phonon_matrix, mode_strength, transfer_mode, energy_offset):
    n = diag_blocks.shape[-1]
    wide = jax.ShapeDtypeStruct((n, 2 * n), F32)
    square = jax.ShapeDtypeStruct((2, n, n), F32)
    left = [jax.ShapeDtypeStruct((n, 2 * n), BF16)] * 2
    right = [jax.ShapeDtypeStruct((2 * n, 2 * n), BF16)] * 2
    flat = [pltpu.VMEM((n, 2 * n), F32)]
    block = [pltpu.VMEM((2, n, n), F32)]
    lefts = [pltpu.VMEM((n, 2 * n), BF16)] * 2
    rights = [pltpu.VMEM((2 * n, 2 * n), BF16)] * 2

    diag_blocks, couplings = [
        pltpu.with_memory_space_constraint(v, pltpu.HBM) for v in (diag_blocks, couplings)
    ]
    *parts, even, border = call(
        first_kernel,
        right + right + left + left + right + [square, wide],
        (diag_blocks, couplings),
        block * 3 + [pltpu.SemaphoreType.DMA((2 * (n // LANES) + 3,))] + lefts * 2 + rights * 2 + flat,
    )
    inverse, slow_right, slow, fast_left, fast_right = [parts[i : i + 2] for i in range(0, 10, 2)]
    border_far = swap(border, "layer", 1)
    *fast, chip = call(
        second_kernel, left + [wide], (even, *inverse, *fast_left, *fast_right)
    )
    chip, border = lax.optimization_barrier((chip, border))
    chip_far = swap(chip, "layer", 0)
    one, two = call(cross_kernel, [wide] * 2, (*slow, *slow_right, *fast, *fast_right))
    scratch = flat + lefts * 2 + rights * 3
    reduced, chip_term = call(chip_kernel, [wide] * 2, (chip, chip_far, one, two), scratch)
    from_border = ahead(chip_term, "layer", 1)
    partial, border_term = call(
        border_kernel, [wide] * 2, (border, border_far, one, two, reduced, chip_term), scratch
    )
    from_chip = ahead(border_term, "layer", 0)
    energies, momenta = lax.axis_size("energy"), lax.axis_size("momentum")
    table = jax.ShapeDtypeStruct((energies * energies + 2 * momenta, LANES), F32)
    (weights,) = call(
        weights_kernel, [table], (phonon_matrix, mode_strength, transfer_mode, energy_offset)
    )
    scratch = flat + lefts + rights * 2
    (greens,) = call(odd_greens_kernel, [square], (partial, from_chip, weights), scratch)
    (greens,) = call(
        even_greens_kernel, [square], (partial, from_border, greens), scratch, aliases={2: 0}
    )
    group = energies * momenta
    depth = 2 * n // group
    axes = ("energy", "momentum")
    spread = lax.all_to_all(
        greens.reshape(group, depth, n), axes, split_axis=0, concat_axis=0, tiled=True
    )
    block = (energies, momenta, depth, n)
    mixed = pl.pallas_call(
        mix_kernel,
        out_shape=jax.ShapeDtypeStruct(block, F32),
        in_specs=[pl.BlockSpec(memory_space=pltpu.VMEM)] * 2,
        out_specs=pl.BlockSpec(memory_space=pltpu.VMEM),
        compiler_params=pltpu.CompilerParams(vmem_limit_bytes=12 * 1024 * 1024),
    )(weights, spread.reshape(block))
    returned = lax.all_to_all(
        mixed.reshape(group, depth, n), axes, split_axis=0, concat_axis=0, tiled=True
    )
    return returned.reshape(1, 1, 1, 2, n, n)


COST = dict(weights_kernel=3 * 10**10, first_kernel=3 * 10**10, second_kernel=3 * 10**10, cross_kernel=3 * 10**10, chip_kernel=3 * 10**10, border_kernel=3 * 10**10, odd_greens_kernel=1, even_greens_kernel=3 * 10**10)


def solution(mesh):
    return jax.shard_map(
        body,
        mesh=mesh,
        in_specs=(
            P("momentum", "layer", "energy", None, None, None),
            P("momentum", "layer", None, None, None),
            P(),
            P(),
            P(),
            P(),
        ),
        out_specs=P("momentum", "layer", "energy", None, None, None),
        check_vma=False,
    )
```

```python
import jax
import jax.numpy as jnp
from jax import lax
from jax.experimental import pallas as pl
from jax.experimental.pallas import tpu as pltpu
from jax.sharding import PartitionSpec as P

F32 = jnp.float32
BF16 = jnp.bfloat16


def split(value):
    high = value.astype(BF16)
    return high, (value - high.astype(F32)).astype(BF16)


LANES = 128


def cut(at):
    return slice(LANES * at, LANES * (at + 1))


def pair(at):
    return slice(2 * LANES * at, 2 * LANES * (at + 1))


def real_of(at):
    return slice(2 * LANES * at, 2 * LANES * at + LANES)


def imag_of(at):
    return slice(2 * LANES * at + LANES, 2 * LANES * (at + 1))


def put_left(left, at, real, imag):
    for columns, part in ((real_of(at), real), (imag_of(at), imag)):
        for ref, value in zip(left, split(part)):
            ref[:, columns] = value


def put_right(right, at, real, imag):
    for ref, r, i in zip(right, split(real), split(imag)):
        minus = -i
        for k in range(real.shape[0] // LANES):
            rows = cut(k)
            ref[real_of(k), real_of(at)] = r[rows]
            ref[real_of(k), imag_of(at)] = i[rows]
            ref[imag_of(k), real_of(at)] = minus[rows]
            ref[imag_of(k), imag_of(at)] = r[rows]


def product(left, right, epilogue, fill=()):
    for at in range(right[0].shape[1] // (2 * LANES)):
        columns = pair(at)
        high = right[0][:, columns]
        lh = left[0][...]
        value = jnp.dot(lh, high, preferred_element_type=F32)
        for low in right[1:]:
            value += jnp.dot(lh, low[:, columns], preferred_element_type=F32)
        for low in left[1:]:
            value += jnp.dot(low[...], high, preferred_element_type=F32)
        if at < len(fill):
            fill[at]()
        epilogue(at, value[:, :LANES], value[:, LANES:])


def storing(out):
    def epilogue(at, real, imag):
        out[:, real_of(at)] = real
        out[:, imag_of(at)] = imag

    return epilogue


def wide_chunk(ref, at):
    return ref[:, real_of(at)], ref[:, imag_of(at)]


def refined_inverse(chunk, left, first, second, rest, epilogue, fill=(), more=()):
    n = rest.shape[0]
    count = n // LANES
    on = lax.broadcasted_iota(jnp.int32, (LANES, LANES), 0) == lax.broadcasted_iota(
        jnp.int32, (LANES, LANES), 1
    )
    eye = on.astype(F32)
    column_parts = []
    for at in range(count):
        real, imag = chunk(at)
        tiles = [jnp.where(on, part[cut(at)], 0.0) for part in (real, imag)]
        pieces = []
        for axis in (0, 1):
            dr, di = [jnp.sum(t, axis=axis, keepdims=True) for t in tiles]
            modulus = dr * dr + di * di
            pieces.append((dr / modulus, -di / modulus))
        (xr, xi), column = pieces
        column_parts.append(column)
        m_real = real * xr - imag * xi
        m_imag = real * xi + imag * xr
        m_real = jnp.concatenate(
            [m_real[cut(k)] - eye if k == at else m_real[cut(k)] for k in range(count)], axis=0
        )
        put_left(left, at, m_real, m_imag)
        put_right(first, at, m_real, m_imag)
        rest[:, real_of(at)] = -m_real
        rest[:, imag_of(at)] = -m_imag

    def square(at, real, imag):
        put_right(second, at, real, imag)
        rest[:, real_of(at)] += real
        rest[:, imag_of(at)] += imag
        rest[cut(at), real_of(at)] += eye

    product(left, first, square, fill)
    col_real, col_imag = [
        jnp.concatenate([c[part] for c in column_parts], axis=0) for part in range(2)
    ]

    def finish(at, real, imag):
        q_real = rest[:, real_of(at)] - real
        q_imag = rest[:, imag_of(at)] - imag
        epilogue(at, col_real * q_real - col_imag * q_imag, col_real * q_imag + col_imag * q_real)

    product(left, second, finish, more)


def pairs_of(refs):
    return [(refs[i], refs[i + 1]) for i in range(0, len(refs), 2)]


def parity():
    return lax.axis_index("layer") % 2


def factors(which, coupling, left, right):
    is_even = which == 0

    def fill(at):
        def run():
            real, imag = coupling[0, :, cut(at)], coupling[1, :, cut(at)]
            real_t, imag_t = coupling[0, cut(at), :].T, -coupling[1, cut(at), :].T
            put_left(left, at, jnp.where(is_even, real, real_t), jnp.where(is_even, imag, imag_t))
            put_right(
                right, at, jnp.where(is_even, real_t, real), jnp.where(is_even, imag_t, imag)
            )

        return run

    return [fill(at) for at in range(coupling.shape[-1] // LANES)]


def sandwich(which, even, left, inverse, right, half, result, fill=()):
    is_even = which == 0
    product(left, inverse, lambda at, real, imag: put_left(half, at, real, imag), fill)

    def finish(at, real, imag):
        for part, (columns, term) in enumerate(((real_of(at), real), (imag_of(at), imag))):
            result[:, columns] = jnp.where(is_even, even[part, :, cut(at)] - term, term)

    product(half, right, finish)


def first_kernel(diag, couplings, *refs):
    inverse, right, half, far_left, far_right = pairs_of(refs[:10])
    even, border, odd, near, far, sems = refs[10:16]
    left, other, first, second = pairs_of(refs[16:24])
    rest = refs[24]
    which = parity()
    count = odd.shape[-1] // LANES
    urgent = [
        pltpu.make_async_copy(
            diag.at[0, 1, 0, part, cut(at)], odd.at[part, cut(at)], sems.at[part * count + at]
        )
        for part in range(2)
        for at in range(count)
    ]
    later = [
        pltpu.make_async_copy(couplings.at[0, which], near, sems.at[2 * count]),
        pltpu.make_async_copy(diag.at[0, 0, 0], even, sems.at[2 * count + 1]),
        pltpu.make_async_copy(couplings.at[0, 1 - which], far, sems.at[2 * count + 2]),
    ]
    for copy in urgent:
        copy.start()

    later[0].start()
    for copy in urgent:
        copy.wait()
    for copy in later[1:]:
        copy.start()

    def chunk(at):
        return odd[0, :, cut(at)], odd[1, :, cut(at)]

    def after(copy, runs):
        def start():
            copy.wait()
            runs[0]()

        return [start] + runs[1:]

    near_fill = factors(which, near, other, right)
    refined_inverse(
        chunk,
        left[:1],
        first[:1],
        second[:1],
        rest,
        lambda at, real, imag: put_right(inverse, at, real, imag),
        [lambda: None, after(later[0], near_fill[:1])[0], near_fill[1]],
        near_fill[2:],
    )
    later[1].wait()
    fill = after(later[2], factors(1 - which, far, far_left, far_right))
    sandwich(which, even, other, inverse, right, half, border, fill)


def second_kernel(even, *refs):
    inverse, left, right, half = pairs_of(refs[:8])
    sandwich(1 - parity(), even, left, inverse, right, half, refs[8])


def cross_kernel(*refs):
    slow, slow_right, fast, fast_right = pairs_of(refs[:8])
    one, two = refs[8:]
    product(slow, fast_right, lambda at, real, imag: storing(one)(at, -real, -imag))
    product(fast, slow_right, lambda at, real, imag: storing(two)(at, -real, -imag))


def reduced_term(chunk, before, after, rest, epilogue, scratch):
    left, other, first, second, third = scratch
    count = before.shape[0] // LANES
    refined_inverse(
        chunk,
        left[:1],
        first[:1],
        second[:1],
        rest,
        lambda at, real, imag: put_right(first, at, real, imag),
        [lambda at=at: put_left(other, at, *wide_chunk(before, at)) for at in range(count)],
        [lambda at=at: put_right(third, at, *wide_chunk(after, at)) for at in range(count)],
    )
    product(other, first, lambda at, real, imag: put_left(left, at, real, imag))
    product(left, third, epilogue)


def chip_kernel(mine, far, one, two, reduced, term, *refs):
    is_even = parity() == 0

    def chunk(at):
        parts = [
            jnp.where(is_even, b - a, a - b)
            for a, b in zip(wide_chunk(mine, at), wide_chunk(far, at))
        ]
        storing(reduced)(at, *parts)
        return parts

    reduced_term(chunk, one, two, refs[0], storing(term), pairs_of(refs[1:]))


def border_kernel(mine, far, one, two, reduced, chip_term, partial, term, *refs):
    index = lax.axis_index("layer")
    is_even = index % 2 == 0
    is_last = index == lax.axis_size("layer") - 1

    def chunk(at):
        parts = [
            jnp.where(is_even, a - b, b - a)
            for a, b in zip(wide_chunk(mine, at), wide_chunk(far, at))
        ]
        for columns, value in zip((real_of(at), imag_of(at)), parts):
            partial[:, columns] = jnp.where(
                is_even, value - chip_term[:, columns], reduced[:, columns]
            )
        return parts

    def finish(at, real, imag):
        for columns, value in ((real_of(at), real), (imag_of(at), imag)):
            value = jnp.where(is_last, 0.0, value)
            term[:, columns] = value
            partial[:, columns] -= jnp.where(is_even, 0.0, value)

    reduced_term(chunk, two, one, refs[0], finish, pairs_of(refs[1:]))


def greens_of(chunk, greens, refs):
    left, first, second = pairs_of(refs[1:])

    def finish(at, real, imag):
        greens[0, :, cut(at)] = real
        greens[1, :, cut(at)] = imag

    refined_inverse(chunk, left, first, second, refs[0], finish)


def weights_kernel(phonon, strength, transfer, offset, weights):
    energies, transfers = phonon.shape[0], transfer.shape[0]

    def put(row, value):
        weights[row : row + 1, :] = jnp.full((1, LANES), value, F32)

    for e in range(energies):
        for f in range(energies):
            put(e * energies + f, phonon[e, f])
    for q in range(transfers):
        mode = transfer[q]
        weight = strength[mode]
        still = offset[mode] == 0
        put(energies * energies + q, jnp.where(still, 2.0 * weight, 0.0))
        put(energies * energies + transfers + q, jnp.where(still, 0.0, weight))


def odd_greens_kernel(partial, chip_term, weights, greens, *refs):
    @pl.when(parity() == 1)
    def _():
        def chunk(at):
            return [a - b for a, b in zip(wide_chunk(partial, at), wide_chunk(chip_term, at))]

        greens_of(chunk, greens, refs)


def even_greens_kernel(partial, border_term, odd_greens, greens, *refs):
    @pl.when(parity() == 0)
    def _():
        def chunk(at):
            return [a - b for a, b in zip(wide_chunk(partial, at), wide_chunk(border_term, at))]

        greens_of(chunk, greens, refs)


def mix_kernel(weights, blocks, mixed):
    momenta, energies, depth, width = blocks.shape
    rows = [weights[row : row + 1, :] for row in range(energies * energies + 2 * momenta)]
    fold = [rows[e * energies : (e + 1) * energies] for e in range(energies)]
    stay, move = rows[-2 * momenta : -momenta], rows[-momenta:]
    for at in range(0, width, 128):
        columns = slice(at, at + 128)

        def rows_of(i, carry):
            rows = pl.ds(pl.multiple_of(i * 8, 8), 8)
            folded = []
            for k in range(momenta):
                g = [blocks[k, f, rows, columns] for f in range(energies)]
                folded.append(
                    [sum(fold[e][f] * g[f] for f in range(energies)) for e in range(energies)]
                )
            for k in range(momenta):
                moved = [
                    sum(move[q] * folded[(k - q) % momenta][e] for q in range(momenta))
                    for e in range(energies)
                ]
                for e in range(energies):
                    total = sum(stay[q] * folded[(k - q) % momenta][e] for q in range(momenta))
                    if e > 0:
                        total = total + moved[e - 1]
                    if e + 1 < energies:
                        total = total + moved[e + 1]
                    mixed[k, e, rows, columns] = total
            return carry

        lax.fori_loop(0, depth // 8, rows_of, 0, unroll=True)


def call(kernel, outs, operands, scratch=(), aliases=()):
    def spec(value):
        if value.ndim > 3:
            return pl.BlockSpec(memory_space=pl.ANY)
        if value.shape[-1] < LANES:
            return pl.BlockSpec(memory_space=pltpu.SMEM)
        return pl.BlockSpec(memory_space=pltpu.VMEM)

    return pl.pallas_call(
        kernel,
        out_shape=outs,
        in_specs=[spec(o) for o in operands],
        out_specs=[spec(o) for o in outs],
        scratch_shapes=list(scratch),
        input_output_aliases=dict(aliases),
        compiler_params=pltpu.CompilerParams(vmem_limit_bytes=20 * 1024 * 1024),
        cost_estimate=pl.CostEstimate(flops=COST[kernel.__name__], bytes_accessed=1, transcendentals=0),
    )(*operands)


def swap(block, axis, first):
    route = []
    for i in range(first, lax.axis_size(axis) - 1, 2):
        route += [(i, i + 1), (i + 1, i)]
    return lax.ppermute(block, axis, route)


def ahead(block, axis, first):
    return lax.ppermute(
        block, axis, [(i, i + 1) for i in range(first, lax.axis_size(axis) - 1, 2)]
    )


def body(diag_blocks, couplings, phonon_matrix, mode_strength, transfer_mode, energy_offset):
    n = diag_blocks.shape[-1]
    wide = jax.ShapeDtypeStruct((n, 2 * n), F32)
    square = jax.ShapeDtypeStruct((2, n, n), F32)
    left = [jax.ShapeDtypeStruct((n, 2 * n), BF16)] * 2
    right = [jax.ShapeDtypeStruct((2 * n, 2 * n), BF16)] * 2
    flat = [pltpu.VMEM((n, 2 * n), F32)]
    block = [pltpu.VMEM((2, n, n), F32)]
    lefts = [pltpu.VMEM((n, 2 * n), BF16)] * 2
    rights = [pltpu.VMEM((2 * n, 2 * n), BF16)] * 2

    diag_blocks, couplings = [
        pltpu.with_memory_space_constraint(v, pltpu.HBM) for v in (diag_blocks, couplings)
    ]
    *parts, even, border = call(
        first_kernel,
        right + right + left + left + right + [square, wide],
        (diag_blocks, couplings),
        block * 3 + [pltpu.SemaphoreType.DMA((2 * (n // LANES) + 3,))] + lefts * 2 + rights * 2 + flat,
    )
    inverse, slow_right, slow, fast_left, fast_right = [parts[i : i + 2] for i in range(0, 10, 2)]
    border_far = swap(border, "layer", 1)
    *fast, chip = call(
        second_kernel, left + [wide], (even, *inverse, *fast_left, *fast_right)
    )
    chip, border = lax.optimization_barrier((chip, border))
    chip_far = swap(chip, "layer", 0)
    one, two = call(cross_kernel, [wide] * 2, (*slow, *slow_right, *fast, *fast_right))
    scratch = flat + lefts * 2 + rights * 3
    reduced, chip_term = call(chip_kernel, [wide] * 2, (chip, chip_far, one, two), scratch)
    from_border = ahead(chip_term, "layer", 1)
    partial, border_term = call(
        border_kernel, [wide] * 2, (border, border_far, one, two, reduced, chip_term), scratch
    )
    from_chip = ahead(border_term, "layer", 0)
    energies, momenta = lax.axis_size("energy"), lax.axis_size("momentum")
    table = jax.ShapeDtypeStruct((energies * energies + 2 * momenta, LANES), F32)
    (weights,) = call(
        weights_kernel, [table], (phonon_matrix, mode_strength, transfer_mode, energy_offset)
    )
    scratch = flat + lefts + rights * 2
    (greens,) = call(odd_greens_kernel, [square], (partial, from_chip, weights), scratch)
    (greens,) = call(
        even_greens_kernel, [square], (partial, from_border, greens), scratch, aliases={2: 0}
    )
    group = energies * momenta
    depth = 2 * n // group
    axes = ("momentum", "energy")
    spread = lax.all_to_all(
        greens.reshape(group, depth, n), axes, split_axis=0, concat_axis=0, tiled=True
    )
    block = (momenta, energies, depth, n)
    mixed = pl.pallas_call(
        mix_kernel,
        out_shape=jax.ShapeDtypeStruct(block, F32),
        in_specs=[pl.BlockSpec(memory_space=pltpu.VMEM)] * 2,
        out_specs=pl.BlockSpec(memory_space=pltpu.VMEM),
        compiler_params=pltpu.CompilerParams(vmem_limit_bytes=12 * 1024 * 1024),
    )(weights, spread.reshape(block))
    returned = lax.all_to_all(
        mixed.reshape(group, depth, n), axes, split_axis=0, concat_axis=0, tiled=True
    )
    return returned.reshape(1, 1, 1, 2, n, n)


COST = dict(weights_kernel=3 * 10**10, first_kernel=3 * 10**10, second_kernel=3 * 10**10, cross_kernel=3 * 10**10, chip_kernel=3 * 10**10, border_kernel=3 * 10**10, odd_greens_kernel=1, even_greens_kernel=3 * 10**10)


def solution(mesh):
    return jax.shard_map(
        body,
        mesh=mesh,
        in_specs=(
            P("momentum", "layer", "energy", None, None, None),
            P("momentum", "layer", None, None, None),
            P(),
            P(),
            P(),
            P(),
        ),
        out_specs=P("momentum", "layer", "energy", None, None, None),
        check_vma=False,
    )
```
